512 devices in a mesh: seq: 32 (over z, core), head: 16 (over x, y).
Axes of the slice: x: 4, y: 4, z: 16, core: 2. Of those that a mesh axis runs over, the one named last changes fastest.
Arguments:
- query_vectors: bfloat16 [65536, 4096], P(('seq', 'head')), may hold values from -6 to 6
- key_vectors: bfloat16 [65536, 4096], P(('seq', 'head')), may hold values from -0.011962891 to 0.011962891
- out_grad: bfloat16 [65536, 4096], P(('seq', 'head')), may hold values from -6 to 6
- log_decay: bfloat16 [65536, 32], P(('seq', 'head')), may hold values from -1 to 0, as said below
- doc_lengths: int32 [8], replicated, may hold values from 1 to 32768, 65536 in all
Outputs:
- value_grad: bfloat16 [65536, 4096], P(('seq', 'head'))
The draws below stay inside these ranges and needn't reach their ends.
Inputs may be any that keep to these rules, and one draw needn't show every extreme that they name: `log_decay`: every entry is negative. `doc_lengths`: the lengths sum to 65536.
All inputs are finite; a program needn't handle non-finite values.
Results may differ from the reference program's by a relative error of at most 0.0043.
Values may be sent and summed in bfloat16 or wider, within the bound.
No kernel may reach another device: no remote copies, remote signals or barrier semaphores. Data moves between devices by JAX's collectives and lax.ppermute only.
A program may use at most 64 MiB of HBM per device.

```python
import math
import jax
import jax.numpy as jnp
import numpy as np
from jax import lax

HD = 128
HEAD_COUNT = 32
DOCS = 8
GROUP = 2048
WINDOW_TOKENS = 65536
BLOCK = 1024


def draw_log_decay(key, part):
    key_pieces = jax.random.split(jax.random.fold_in(key, 17), 9)
    steady_count = HEAD_COUNT // 2
    head_order = jax.random.permutation(key_pieces[0], HEAD_COUNT)
    steady_heads = head_order < steady_count
    steady_rate = jnp.exp(jax.random.uniform(key_pieces[1], (HEAD_COUNT,), jnp.float32, jnp.log(0.05 / WINDOW_TOKENS), jnp.log(0.5 / WINDOW_TOKENS)))
    switch_count = WINDOW_TOKENS // (2 * GROUP)
    switch_points = jax.random.randint(key_pieces[2], (switch_count, HEAD_COUNT), 1, WINDOW_TOKENS)
    token_positions = jnp.arange(WINDOW_TOKENS, dtype=jnp.int32)
    stretch_index = jnp.zeros((WINDOW_TOKENS, HEAD_COUNT), jnp.int32)
    for switch_number in range(switch_count):
        passed = switch_points[switch_number][None, :] <= token_positions[:, None]
        stretch_index = stretch_index + passed.astype(jnp.int32)
    start_fast = jax.random.randint(key_pieces[3], (HEAD_COUNT,), 0, 2)
    fast_now = (stretch_index + start_fast[None, :]) % 2 == 1
    stretch_fast = jnp.exp(jax.random.uniform(key_pieces[4], (switch_count + 1, HEAD_COUNT), jnp.float32, jnp.log(0.2 / GROUP), jnp.log(1.0 / 30.0)))
    stretch_slow = jnp.exp(jax.random.uniform(key_pieces[5], (switch_count + 1, HEAD_COUNT), jnp.float32, jnp.log(0.05 / WINDOW_TOKENS), jnp.log(0.5 / WINDOW_TOKENS)))
    fast_rows = jnp.take_along_axis(stretch_fast, stretch_index, axis=0)
    slow_rows = jnp.take_along_axis(stretch_slow, stretch_index, axis=0)
    switching_rate = jnp.where(fast_now, fast_rows, slow_rows)
    head_rate = jnp.where(steady_heads[None, :], steady_rate[None, :], switching_rate)
    rough = jnp.exp(jax.random.uniform(key_pieces[6], (WINDOW_TOKENS, HEAD_COUNT), jnp.float32, jnp.log(0.5), jnp.log(2.0)))
    value_rows = -head_rate * rough
    spike_position = jax.random.randint(key_pieces[7], (2,), 0, WINDOW_TOKENS)
    spike_loss_term = jax.random.uniform(key_pieces[8], (2, HEAD_COUNT), jnp.float32, 0.2, 0.5)
    spike_logarithm = jnp.log1p(-spike_loss_term)
    matched_rows = token_positions[:, None] == spike_position[None, :]
    value_rows = value_rows + jnp.sum(jnp.where(matched_rows[:, :, None], spike_logarithm[None, :, :], 0.0), axis=1)
    return value_rows.astype(jnp.bfloat16)


def shard_levels(rng, extent, cuts, smallest, largest):
    loudness, own = 1.0, jax.random.fold_in(rng, 6)
    for position, parts in cuts:
        steps = jnp.exp(jax.random.uniform(jax.random.fold_in(own, position), (parts,), jnp.float32, smallest / len(cuts), largest / len(cuts)))
        loudness = loudness * jnp.repeat(steps, extent[position] // parts).reshape([-1 if axis == position else 1 for axis in range(len(extent))])
    return loudness


def split_up(count, total, most, skew):
    portions = [(1 << 20) // math.isqrt(standing ** skew) + 1 for standing in range(2, count + 1)]
    spare, given = total - most - (count - 1), [1] * (count - 1)
    while spare > 0:
        movable = [i for i in range(count - 1) if given[i] < most]
        whole, remaining = sum([portions[i] for i in movable]), spare
        for i in movable:
            extra = min(most - given[i], max(1, remaining * portions[i] // whole), spare)
            given[i] = given[i] + extra
            spare = spare - extra
    return np.array([most] + given)


def uneven_parts(rng, count, total, bound, slope):
    if count == 2:
        one = jax.random.randint(rng, (), max(1, total - bound), min(bound, total - 1) + 1)
        return jnp.stack([one, total - one])
    sizes = jnp.asarray(split_up(count, total, bound, slope), jnp.int32)
    couples = (count - 1) // 2
    source_of, taker = sizes[1:1 + 2 * couples:2], sizes[2:2 + 2 * couples:2]
    margin = jnp.minimum(source_of - 1, bound - taker)
    moved = jax.random.randint(jax.random.fold_in(rng, 1), (couples,), 0, 1 << 20) % (margin + 1)
    sizes = sizes.at[1:1 + 2 * couples:2].set(source_of - moved).at[2:2 + 2 * couples:2].set(taker + moved)
    return sizes[jax.random.permutation(jax.random.fold_in(rng, 2), count)]


def scatter_about(key, dims, deviation, limit, cuts=(), kind=jnp.bfloat16):
    entries = jax.random.normal(key, dims, jnp.float32) * deviation
    if len(cuts) > 0:
        entries = shard_levels(key, dims, cuts, -0.22, 0.18) * entries
    return jnp.clip(entries, min=-limit, max=limit).astype(kind)


def setup_inputs(seed: int = 0) -> dict:
    arg_keys = jax.random.split(jax.random.key(seed), 6)
    return {
        "query_vectors": scatter_about(arg_keys[0], (WINDOW_TOKENS, HEAD_COUNT * HD), 1.0, 6.0, ((0, 512),)),
        "key_vectors": scatter_about(arg_keys[1], (WINDOW_TOKENS, HEAD_COUNT * HD), 0.002, 0.011962891, ((0, 512),)),
        "out_grad": scatter_about(arg_keys[2], (WINDOW_TOKENS, HEAD_COUNT * HD), 1.0, 6.0, ((0, 512),)),
        "log_decay": draw_log_decay(jax.random.fold_in(arg_keys[5], 71), 0),
        "doc_lengths": uneven_parts(arg_keys[4], DOCS, WINDOW_TOKENS, WINDOW_TOKENS // 2, 2).astype(jnp.int32),
    }


def segment_ids(token_positions, doc_starts):
    return jnp.sum((doc_starts[None, :] <= token_positions[:, None]).astype(jnp.int32), axis=1)


def reference(query_vectors, key_vectors, out_grad, log_decay, doc_lengths):
    blocks = WINDOW_TOKENS // BLOCK
    highest = lax.Precision.HIGHEST
    doc_starts = (jnp.cumsum(doc_lengths) - doc_lengths).astype(jnp.int32)
    query_blocks = query_vectors.reshape(blocks, BLOCK, HEAD_COUNT, HD)
    key_blocks = key_vectors.reshape(blocks, BLOCK, HEAD_COUNT, HD)
    grad_blocks = out_grad.reshape(blocks, BLOCK, HEAD_COUNT, HD)
    decay_blocks = log_decay.reshape(blocks, BLOCK, HEAD_COUNT)
    offsets = jnp.arange(BLOCK, dtype=jnp.int32)
    causal = offsets[None, :] >= offsets[:, None]

    def block_step(state, inputs):
        queries, key_rows, grads, decays, block_index = inputs
        token_positions = block_index * BLOCK + offsets
        segments = segment_ids(token_positions, doc_starts)
        before = segment_ids(token_positions[:1] - 1, doc_starts)[0]
        cumulative = jnp.cumsum(decays.astype(jnp.float32), axis=0)
        query_float = queries.astype(jnp.float32)
        key_float = key_rows.astype(jnp.float32)
        grad_float = grads.astype(jnp.float32)
        scores = jnp.einsum("ihe,the->hit", key_float, query_float, precision=highest)
        by_head = cumulative.T
        decay_gaps = by_head[:, None, :] - by_head[:, :, None]
        allowed = causal & (segments[None, :] == segments[:, None])
        weights = (jnp.where(allowed[None], jnp.exp(jnp.minimum(decay_gaps, 0.0)), 0.0) * scores).astype(jnp.bfloat16)
        inside = jnp.einsum("hit,the->ihe", weights.astype(jnp.float32), grad_float, precision=highest)
        last_segment = segments[-1]
        last_cum = cumulative[-1]
        tail_weight = jnp.where((segments == last_segment)[:, None], jnp.exp(last_cum[None, :] - cumulative), 0.0)
        carried = jnp.einsum("ihe,hef->ihf", key_float, state, precision=highest) * tail_weight[:, :, None]
        value_grad = (inside + carried).astype(jnp.bfloat16)
        linked = segments == before
        scaled = (jnp.where(linked[:, None], jnp.exp(cumulative), 0.0)[:, :, None] * query_float).astype(jnp.bfloat16)
        summary = jnp.einsum("the,thf->hef", scaled.astype(jnp.float32), grad_float, precision=highest)
        factor = jnp.where(last_segment == before, jnp.exp(last_cum), 0.0)
        new_state = summary + factor[:, None, None] * state
        return new_state, value_grad

    initial = jnp.zeros((HEAD_COUNT, HD, HD), jnp.float32)
    final_state, grads_out = lax.scan(block_step, initial, (query_blocks, key_blocks, grad_blocks, decay_blocks, jnp.arange(blocks, dtype=jnp.int32)), reverse=True)
    return grads_out.reshape(WINDOW_TOKENS, HEAD_COUNT * HD)
```

```python
import jax
import jax.numpy as jnp
from jax import lax
from jax.experimental import pallas as pl
from jax.experimental.pallas import tpu as pltpu
from jax.sharding import Mesh, PartitionSpec as P

HEAD = 128
PAD = 16
NEG = -1e30
PLANE = ("core", "x", "y")


def token_segments(lengths_ref, positions):
    start = jnp.int32(0)
    total = jnp.zeros(positions.shape, jnp.int32)
    for d in range(lengths_ref.shape[0]):
        total = total + (start <= positions).astype(jnp.int32)
        start = start + lengths_ref[d]
    return total


def scalar_segment(lengths_ref, position):
    start = jnp.int32(0)
    total = jnp.int32(0)
    for d in range(lengths_ref.shape[0]):
        total = total + (start <= position).astype(jnp.int32)
        start = start + lengths_ref[d]
    return total


def running_sum(decay):
    rows = decay.shape[0]
    later = lax.broadcasted_iota(jnp.int32, (rows, rows), 0) >= lax.broadcasted_iota(jnp.int32, (rows, rows), 1)
    return jnp.dot(later.astype(jnp.bfloat16), decay, preferred_element_type=jnp.float32)


def running_sum_rows(decay):
    rows = decay.shape[0]
    earlier = lax.broadcasted_iota(jnp.int32, (rows, rows), 0) <= lax.broadcasted_iota(jnp.int32, (rows, rows), 1)
    return lax.dot_general(
        decay, earlier.astype(jnp.bfloat16), (((0,), (0,)), ((), ())), preferred_element_type=jnp.float32
    )


def summary_kernel(lengths_ref, base_ref, q_ref, g_ref, decay_ref, out_ref):
    rows = q_ref.shape[0]
    heads = decay_ref.shape[1]
    base = base_ref[0]
    cum = running_sum(decay_ref[...])
    before = scalar_segment(lengths_ref, base - 1)
    last = scalar_segment(lengths_ref, base + rows - 1)
    seg = token_segments(lengths_ref, base + lax.broadcasted_iota(jnp.int32, (rows, heads), 0))
    scale = jnp.where(seg == before, jnp.exp(cum), 0.0)
    factor = jnp.where(last == before, jnp.exp(cum[rows - 1 : rows, :]), 0.0)
    f_hi = factor.astype(jnp.bfloat16)
    rest = factor - f_hi.astype(jnp.float32)
    f_mid = rest.astype(jnp.bfloat16)
    f_lo = (rest - f_mid.astype(jnp.float32)).astype(jnp.bfloat16)
    which = lax.broadcasted_iota(jnp.int32, (PAD, HEAD), 0)
    for h in range(heads):
        cols = slice(h * HEAD, (h + 1) * HEAD)
        scaled = q_ref[:, cols].astype(jnp.float32) * scale[:, h : h + 1]
        hi = scaled.astype(jnp.bfloat16)
        lo = (scaled - hi.astype(jnp.float32)).astype(jnp.bfloat16)
        g_t = g_ref[:, cols].T
        summary = jnp.dot(
            jnp.concatenate([g_t, g_t], axis=1),
            jnp.concatenate([hi, lo], axis=0),
            preferred_element_type=jnp.float32,
        )
        out_ref[h, 0:HEAD, :] = summary.astype(jnp.bfloat16)
        parts = [jnp.broadcast_to(f[:, h : h + 1].astype(jnp.float32), (PAD, HEAD)) for f in (f_hi, f_mid, f_lo)]
        tail = jnp.where(which == 0, parts[0], jnp.where(which == 1, parts[1], jnp.where(which == 2, parts[2], 0.0)))
        out_ref[h, HEAD : HEAD + PAD, :] = tail.astype(jnp.bfloat16)


def inside_kernel(lengths_ref, base_ref, q_ref, k_ref, g_ref, decay_ref, out_ref):
    rows = q_ref.shape[0]
    heads = decay_ref.shape[1]
    base = base_ref[0]
    cum = running_sum(decay_ref[...])
    cum_rows = running_sum_rows(decay_ref[...])
    i_pos = lax.broadcasted_iota(jnp.int32, (rows, rows), 0)
    t_pos = lax.broadcasted_iota(jnp.int32, (rows, rows), 1)
    same = token_segments(lengths_ref, base + i_pos) == token_segments(lengths_ref, base + t_pos)
    bias = jnp.where(same & (t_pos >= i_pos), 0.0, NEG)
    for h in range(heads):
        cols = slice(h * HEAD, (h + 1) * HEAD)
        scores = lax.dot_general(
            k_ref[:, cols], q_ref[:, cols], (((1,), (1,)), ((), ())), preferred_element_type=jnp.float32
        )
        gaps = jnp.minimum(cum_rows[h : h + 1, :] - cum[:, h : h + 1], 0.0)
        weights = (jnp.exp(gaps + bias) * scores).astype(jnp.bfloat16)
        out_ref[:, cols] = jnp.dot(weights, g_ref[:, cols], preferred_element_type=jnp.float32)


def factor_row(ref, p):
    tail = ref[p, HEAD : HEAD + PAD, :].astype(jnp.float32)
    return tail[0:1, :] + tail[1:2, :] + tail[2:3, :]


def reduce_kernel(parts_ref, out_ref):
    count = parts_ref.shape[0]
    state = jnp.zeros((HEAD, HEAD), jnp.float32)
    factor = jnp.ones((1, HEAD), jnp.float32)
    for p in reversed(range(count)):
        f = factor_row(parts_ref, p)
        state = parts_ref[p, 0:HEAD, :].astype(jnp.float32) + f * state
        factor = factor * f
    out_ref[0:HEAD, :] = state
    out_ref[HEAD : HEAD + 8, :] = jnp.broadcast_to(factor, (8, HEAD))


def join_kernel(own_ref, a_ref, b_ref, c_ref, near_ref, wide_ref):
    def read(ref):
        return ref[0:HEAD, :], ref[HEAD : HEAD + 1, :]

    s0, f0 = read(own_ref)
    s1, f1 = read(a_ref)
    s2, f2 = read(b_ref)
    s3, f3 = read(c_ref)
    near = s1 + f1 * (s2 + f2 * s3)
    near_f = f1 * f2 * f3
    near_ref[0:HEAD, :] = near
    near_ref[HEAD : HEAD + 8, :] = jnp.broadcast_to(near_f, (8, HEAD))
    wide_ref[0:HEAD, :] = s0 + f0 * near
    wide_ref[HEAD : HEAD + 8, :] = jnp.broadcast_to(f0 * near_f, (8, HEAD))


def states_kernel(parts_ref, near_ref, a_ref, b_ref, c_ref, out_ref):
    def read(ref):
        return ref[0:HEAD, :], ref[HEAD : HEAD + 1, :]

    s0, f0 = read(near_ref)
    s1, f1 = read(a_ref)
    s2, f2 = read(b_ref)
    s3, f3 = read(c_ref)
    state = s0 + f0 * (s1 + f1 * (s2 + f2 * s3))
    for p in reversed(range(parts_ref.shape[0])):
        out_ref[p] = state.astype(jnp.bfloat16)
        state = parts_ref[p, 0:HEAD, :].astype(jnp.float32) + factor_row(parts_ref, p) * state


def output_kernel(lengths_ref, base_ref, k_ref, decay_ref, inside_ref, states_ref, out_ref):
    rows = k_ref.shape[0]
    heads = decay_ref.shape[1]
    base = base_ref[0]
    cum = running_sum(decay_ref[...])
    last = scalar_segment(lengths_ref, base + rows - 1)
    seg = token_segments(lengths_ref, base + lax.broadcasted_iota(jnp.int32, (rows, heads), 0))
    tail = jnp.where(seg == last, jnp.exp(cum[rows - 1 : rows, :] - cum), 0.0)
    for h in range(heads):
        cols = slice(h * HEAD, (h + 1) * HEAD)
        carried = lax.dot_general(
            k_ref[:, cols], states_ref[h], (((1,), (1,)), ((), ())), preferred_element_type=jnp.float32
        )
        out_ref[:, cols] = (inside_ref[:, cols] + tail[:, h : h + 1] * carried).astype(jnp.bfloat16)


def call(kernel, out_shape, scalars, arrays):
    smem = pl.BlockSpec(memory_space=pltpu.SMEM)
    vmem = pl.BlockSpec(memory_space=pltpu.VMEM)
    single = not isinstance(out_shape, (list, tuple))
    return pl.pallas_call(
        kernel,
        out_shape=out_shape,
        in_specs=[smem] * len(scalars) + [vmem] * len(arrays),
        out_specs=vmem if single else [vmem] * len(out_shape),
        compiler_params=pltpu.CompilerParams(vmem_limit_bytes=48 * 1024 * 1024),
    )(*scalars, *arrays)


def from_ahead(x, by):
    size = lax.axis_size("z")
    return lax.ppermute(x, "z", [(i + by, i) for i in range(size - by)])


def body(query_vectors, key_vectors, out_grad, log_decay, doc_lengths):
    rows, heads = log_decay.shape
    index = lax.axis_index(("z", "core", "x", "y"))
    base = (index * rows).astype(jnp.int32).reshape(1)
    scalars = (doc_lengths, base)
    shape = jax.ShapeDtypeStruct
    summaries = call(
        summary_kernel,
        shape((heads, HEAD + PAD, HEAD), jnp.bfloat16),
        scalars,
        (query_vectors, out_grad, log_decay),
    )
    parts = lax.all_to_all(summaries, PLANE, split_axis=0, concat_axis=0, tiled=True)
    inside = call(
        inside_kernel,
        shape(query_vectors.shape, jnp.float32),
        scalars,
        (query_vectors, key_vectors, out_grad, log_decay),
    )
    pair = shape((HEAD + 8, HEAD), jnp.float32)
    plane_total = call(reduce_kernel, pair, (), (parts,))
    ahead = [from_ahead(plane_total, by) for by in (1, 2, 3)]
    near, wide = call(join_kernel, (pair, pair), (), (plane_total, *ahead))
    far = [from_ahead(wide, by) for by in (4, 8, 12)]
    states = call(states_kernel, shape((heads, HEAD, HEAD), jnp.bfloat16), (), (parts, near, *far))
    mine = lax.all_to_all(states, PLANE, split_axis=0, concat_axis=0, tiled=True)
    return call(
        output_kernel,
        shape(query_vectors.shape, jnp.bfloat16),
        scalars,
        (key_vectors, log_decay, inside, mine),
    )


def solution(mesh):
    side = 4
    fine = Mesh(
        mesh.devices.reshape(mesh.shape["seq"] // 2, 2, side, mesh.shape["head"] // side), ("z", "core", "x", "y")
    )
    tokens = P(("z", "core", "x", "y"), None)
    return jax.shard_map(
        body, mesh=fine, in_specs=(tokens, tokens, tokens, tokens, P()), out_specs=tokens, check_vma=False
    )
```

```python
import jax
import jax.numpy as jnp
from jax import lax
from jax.experimental import pallas as pl
from jax.experimental.pallas import tpu as pltpu
from jax.sharding import Mesh, PartitionSpec as P

HEAD = 128
PAD = 16
NEG = -1e30
TINY = 1e-36
OCTAVES = 120.0
GROUPS = 4
PLANE = ("core", "x", "y")


def token_segments(lengths_ref, positions):
    start = jnp.int32(0)
    total = jnp.zeros(positions.shape, jnp.int32)
    for d in range(lengths_ref.shape[0]):
        total = total + (start <= positions).astype(jnp.int32)
        start = start + lengths_ref[d]
    return total


def scalar_segment(lengths_ref, position):
    start = jnp.int32(0)
    total = jnp.int32(0)
    for d in range(lengths_ref.shape[0]):
        total = total + (start <= position).astype(jnp.int32)
        start = start + lengths_ref[d]
    return total


def running_sums(decay_rows):
    size = decay_rows.shape[1]
    upto = lax.broadcasted_iota(jnp.int32, (size, size), 0) <= lax.broadcasted_iota(jnp.int32, (size, size), 1)
    by_row = jnp.dot(decay_rows, upto.astype(jnp.bfloat16), preferred_element_type=jnp.float32)
    since = lax.broadcasted_iota(jnp.int32, (size, size), 0) >= lax.broadcasted_iota(jnp.int32, (size, size), 1)
    by_col = lax.dot_general(
        since.astype(jnp.bfloat16), decay_rows, (((1,), (1,)), ((), ())), preferred_element_type=jnp.float32
    )
    return by_row, by_col


def split3(value):
    hi = value.astype(jnp.bfloat16)
    rest = value - hi.astype(jnp.float32)
    mid = rest.astype(jnp.bfloat16)
    lo = (rest - mid.astype(jnp.float32)).astype(jnp.bfloat16)
    return [part.astype(jnp.float32) for part in (hi, mid, lo)]


def pad_rows(rows):
    which = lax.broadcasted_iota(jnp.int32, (PAD, HEAD), 0)
    out = jnp.zeros((PAD, HEAD), jnp.float32)
    for number, row in enumerate(rows):
        out = jnp.where(which == number, jnp.broadcast_to(row, (PAD, HEAD)), out)
    return out.astype(jnp.bfloat16)


def summary_kernel(
    base_ref, lengths_hbm, q_hbm, g_hbm, decay_hbm, out_ref, q_buf, g_buf, decay_ref, lengths_ref, sems, small_sems
):
    rows = q_buf.shape[0]
    heads = decay_ref.shape[0]
    groups = sems.shape[1]
    width = q_buf.shape[1] // groups
    small = [
        pltpu.make_async_copy(lengths_hbm, lengths_ref, small_sems.at[0]),
        pltpu.make_async_copy(decay_hbm, decay_ref, small_sems.at[1]),
    ]
    for copy in small:
        copy.start()
    large = []
    for n in range(groups):
        span = slice(n * width, (n + 1) * width)
        pair = [
            pltpu.make_async_copy(q_hbm.at[:, span], q_buf.at[:, span], sems.at[0, n]),
            pltpu.make_async_copy(g_hbm.at[:, span], g_buf.at[:, span], sems.at[1, n]),
        ]
        for copy in pair:
            copy.start()
        large.append(pair)
    for copy in small:
        copy.wait()
    base = base_ref[0]
    by_row, cum = running_sums(decay_ref[...])
    before = scalar_segment(lengths_ref, base - 1)
    last = scalar_segment(lengths_ref, base + rows - 1)
    seg = token_segments(lengths_ref, base + lax.broadcasted_iota(jnp.int32, (rows, heads), 0))
    scale = jnp.where(seg == before, jnp.exp(cum), 0.0)
    factors = split3(jnp.where(last == before, jnp.exp(cum[rows - 1 : rows, :]), 0.0))
    for h in range(heads):
        cols = slice(h * HEAD, (h + 1) * HEAD)
        if (h * HEAD) % width == 0:
            for copy in large[h * HEAD // width]:
                copy.wait()
        scaled = q_buf[:, cols].astype(jnp.float32) * scale[:, h : h + 1]
        hi = scaled.astype(jnp.bfloat16)
        lo = (scaled - hi.astype(jnp.float32)).astype(jnp.bfloat16)
        g_t = g_buf[:, cols].T
        summary = jnp.dot(
            jnp.concatenate([g_t, g_t], axis=1),
            jnp.concatenate([hi, lo], axis=0),
            preferred_element_type=jnp.float32,
        )
        out_ref[h, 0:HEAD, :] = summary.astype(jnp.bfloat16)
        out_ref[h, HEAD : HEAD + PAD, :] = pad_rows([f[:, h : h + 1] for f in factors])


def inside_kernel(
    base_ref, lengths_ref, q_ref, k_ref, g_ref, decay_ref, after_ref, inside_ref, tail_ref, keys_ref
):
    rows = q_ref.shape[0]
    heads = decay_ref.shape[0]
    base = base_ref[0]
    cum_rows, cum = running_sums(decay_ref[...])
    last = scalar_segment(lengths_ref, base + rows - 1)
    seg = token_segments(lengths_ref, base + lax.broadcasted_iota(jnp.int32, (rows, heads), 0))
    tail_ref[...] = jnp.where(seg == last, jnp.exp(cum[rows - 1 : rows, :] - cum), 0.0)
    i_pos = lax.broadcasted_iota(jnp.int32, (rows, rows), 0)
    t_pos = lax.broadcasted_iota(jnp.int32, (rows, rows), 1)
    same = token_segments(lengths_ref, base + i_pos) == token_segments(lengths_ref, base + t_pos)
    bias = jnp.where(same & (t_pos >= i_pos), 0.0, NEG)
    for h in range(heads):
        cols = slice(h * HEAD, (h + 1) * HEAD)
        keys = k_ref[:, cols]
        keys_ref[:, cols] = keys
        scores = lax.dot_general(
            keys, q_ref[:, cols], (((1,), (1,)), ((), ())), preferred_element_type=jnp.float32
        )
        gaps = jnp.minimum(cum_rows[h : h + 1, :] - cum[:, h : h + 1], 0.0)
        weights = (jnp.exp(gaps + bias) * scores).astype(jnp.bfloat16)
        inside_ref[:, cols] = jnp.dot(weights, g_ref[:, cols], preferred_element_type=jnp.float32)


def factor_row(ref, p):
    tail = ref[p, HEAD : HEAD + PAD, :].astype(jnp.float32)
    return tail[0:1, :] + tail[1:2, :] + tail[2:3, :]


def write_packet(ref, state, factor):
    size = jnp.abs(state)
    largest = jnp.max(jnp.max(size, axis=0, keepdims=True), axis=1, keepdims=True)
    bound = (largest * 1.01 + TINY).astype(jnp.bfloat16).astype(jnp.float32)
    code = jnp.exp2(size * ((2.0 * OCTAVES) / bound) - OCTAVES)
    ref[0:HEAD, :] = jnp.where(state < 0.0, -code, code).astype(jnp.bfloat16)
    ref[HEAD : HEAD + PAD, :] = pad_rows([bound] + split3(factor))


def read_packet(ref):
    code = ref[0:HEAD, :].astype(jnp.float32)
    tail = ref[HEAD : HEAD + PAD, :].astype(jnp.float32)
    octaves = jnp.log2(jnp.maximum(jnp.abs(code), 2.0**-OCTAVES)) + OCTAVES
    size = octaves * (tail[0:1, :] * (0.5 / OCTAVES))
    return jnp.where(code < 0.0, -size, size), tail[1:2, :] + tail[2:3, :] + tail[3:4, :]


def reduce_kernel(parts_ref, total_ref, factor_ref, packet_ref):
    state = jnp.zeros((HEAD, HEAD), jnp.float32)
    factor = jnp.ones((1, HEAD), jnp.float32)
    for p in reversed(range(parts_ref.shape[0])):
        f = factor_row(parts_ref, p)
        state = parts_ref[p, 0:HEAD, :].astype(jnp.float32) + f * state
        factor = factor * f
    total_ref[...] = state
    factor_ref[...] = factor
    write_packet(packet_ref, state, factor)


def join(refs):
    state, factor = read_packet(refs[-1])
    for ref in reversed(refs[:-1]):
        s, f = read_packet(ref)
        state = s + f * state
        factor = f * factor
    return state, factor


def join_kernel(total_ref, factor_ref, a_ref, b_ref, c_ref, near_ref, near_factor_ref, packet_ref):
    state, factor = join([a_ref, b_ref, c_ref])
    near_ref[...] = state
    near_factor_ref[...] = factor
    own = factor_ref[...]
    write_packet(packet_ref, total_ref[...] + own * state, own * factor)


def states_kernel(parts_ref, near_ref, near_factor_ref, a_ref, b_ref, c_ref, after_ref, out_ref):
    far, far_factor = join([a_ref, b_ref, c_ref])
    state = near_ref[...] + near_factor_ref[...] * far
    for p in reversed(range(parts_ref.shape[0])):
        out_ref[p] = state.astype(jnp.bfloat16)
        state = parts_ref[p, 0:HEAD, :].astype(jnp.float32) + factor_row(parts_ref, p) * state


def output_kernel(keys_ref, tail_ref, inside_ref, states_ref, out_hbm, out_buf, sems):
    groups = sems.shape[0]
    width = out_buf.shape[1] // groups
    tail = tail_ref[...]
    copies = []
    for h in range(states_ref.shape[0]):
        cols = slice(h * HEAD, (h + 1) * HEAD)
        carried = lax.dot_general(
            keys_ref[:, cols], states_ref[h], (((1,), (1,)), ((), ())), preferred_element_type=jnp.float32
        )
        out_buf[:, cols] = (inside_ref[:, cols] + tail[:, h : h + 1] * carried).astype(jnp.bfloat16)
        if ((h + 1) * HEAD) % width == 0:
            n = h * HEAD // width
            span = slice(n * width, (n + 1) * width)
            copies.append(pltpu.make_async_copy(out_buf.at[:, span], out_hbm.at[:, span], sems.at[n]))
            copies[-1].start()
    for copy in copies:
        copy.wait()


SMEM = pl.BlockSpec(memory_space=pltpu.SMEM)
VMEM = pl.BlockSpec(memory_space=pltpu.VMEM)
REST = pl.BlockSpec(memory_space=pltpu.HBM)


def call(kernel, out_shape, in_specs, args, out_specs=None, scratch=()):
    if out_specs is None:
        out_specs = [VMEM] * len(out_shape) if isinstance(out_shape, (list, tuple)) else VMEM
    return pl.pallas_call(
        kernel,
        out_shape=out_shape,
        in_specs=in_specs,
        out_specs=out_specs,
        scratch_shapes=list(scratch),
        compiler_params=pltpu.CompilerParams(vmem_limit_bytes=40 * 1024 * 1024),
    )(*args)


def from_ahead(x, by):
    size = lax.axis_size("z")
    return lax.ppermute(x, "z", [(i + by, i) for i in range(size - by)])


def body(query_vectors, key_vectors, out_grad, log_decay, doc_lengths):
    rows, heads = log_decay.shape
    columns = query_vectors.shape[1]
    index = lax.axis_index(("z", "core", "x", "y"))
    base = (index * rows).astype(jnp.int32).reshape(1)
    decay_rows = log_decay.T
    shape = jax.ShapeDtypeStruct
    dma = pltpu.SemaphoreType.DMA
    summaries = call(
        summary_kernel,
        shape((heads, HEAD + PAD, HEAD), jnp.bfloat16),
        [SMEM] + [REST] * 4,
        (base, doc_lengths, query_vectors, out_grad, decay_rows),
        scratch=(
            pltpu.VMEM((rows, columns), jnp.bfloat16),
            pltpu.VMEM((rows, columns), jnp.bfloat16),
            pltpu.VMEM((heads, rows), jnp.bfloat16),
            pltpu.SMEM(doc_lengths.shape, jnp.int32),
            dma((2, GROUPS)),
            dma((2,)),
        ),
    )
    parts = lax.all_to_all(summaries, PLANE, split_axis=0, concat_axis=0, tiled=True)
    state = shape((HEAD, HEAD), jnp.float32)
    factor = shape((1, HEAD), jnp.float32)
    packet = shape((HEAD + PAD, HEAD), jnp.bfloat16)
    total, total_factor, own = call(reduce_kernel, (state, factor, packet), [VMEM], (parts,))
    ahead = [from_ahead(own, by) for by in (1, 2, 3)]
    near, near_factor, wide = call(
        join_kernel, (state, factor, packet), [VMEM] * 5, (total, total_factor, *ahead)
    )
    far = [from_ahead(wide, by) for by in (4, 8, 12)]
    inside, tail, keys = call(
        inside_kernel,
        (
            shape((rows, columns), jnp.float32),
            shape((rows, heads), jnp.float32),
            shape((rows, columns), jnp.bfloat16),
        ),
        [SMEM] * 2 + [VMEM] * 5,
        (base, doc_lengths, query_vectors, key_vectors, out_grad, decay_rows, wide),
    )
    states = call(
        states_kernel,
        shape((heads, HEAD, HEAD), jnp.bfloat16),
        [VMEM] * 7,
        (parts, near, near_factor, *far, tail),
    )
    mine = lax.all_to_all(states, PLANE, split_axis=0, concat_axis=0, tiled=True)
    return call(
        output_kernel,
        shape((rows, columns), jnp.bfloat16),
        [VMEM] * 4,
        (keys, tail, inside, mine),
        out_specs=REST,
        scratch=(pltpu.VMEM((rows, columns), jnp.bfloat16), dma((GROUPS,))),
    )


def solution(mesh):
    side = 4
    fine = Mesh(
        mesh.devices.reshape(mesh.shape["seq"] // 2, 2, side, mesh.shape["head"] // side), ("z", "core", "x", "y")
    )
    tokens = P(("z", "core", "x", "y"), None)
    return jax.shard_map(
        body, mesh=fine, in_specs=(tokens, tokens, tokens, tokens, P()), out_specs=tokens, check_vma=False
    )
```

```python
import functools
import jax
import jax.numpy as jnp
from jax import lax
from jax.experimental import pallas as pl
from jax.experimental.pallas import tpu as pltpu
from jax.sharding import Mesh, PartitionSpec as P

HEAD = 128
PAD = 8
HALF = 64
NEG = -1e30
TINY = 1e-36
OCTAVES = 120.0
GROUPS = 4
GROUP = ("zl", "core", "x", "y")


def token_segments(lengths_ref, positions):
    start = jnp.int32(0)
    total = jnp.zeros(positions.shape, jnp.int32)
    for d in range(lengths_ref.shape[0]):
        total = total + (start <= positions).astype(jnp.int32)
        start = start + lengths_ref[d]
    return total


def scalar_segment(lengths_ref, position):
    start = jnp.int32(0)
    total = jnp.int32(0)
    for d in range(lengths_ref.shape[0]):
        total = total + (start <= position).astype(jnp.int32)
        start = start + lengths_ref[d]
    return total


def running_sums(decay_rows):
    size = decay_rows.shape[1]
    upto = lax.broadcasted_iota(jnp.int32, (size, size), 0) <= lax.broadcasted_iota(jnp.int32, (size, size), 1)
    by_row = jnp.dot(decay_rows, upto.astype(jnp.bfloat16), preferred_element_type=jnp.float32)
    since = lax.broadcasted_iota(jnp.int32, (size, size), 0) >= lax.broadcasted_iota(jnp.int32, (size, size), 1)
    by_col = lax.dot_general(
        since.astype(jnp.bfloat16), decay_rows, (((1,), (1,)), ((), ())), preferred_element_type=jnp.float32
    )
    return by_row, by_col


def split3(value):
    hi = value.astype(jnp.bfloat16)
    rest = value - hi.astype(jnp.float32)
    mid = rest.astype(jnp.bfloat16)
    lo = (rest - mid.astype(jnp.float32)).astype(jnp.bfloat16)
    return [part.astype(jnp.float32) for part in (hi, mid, lo)]


def pad_rows(rows):
    which = lax.broadcasted_iota(jnp.int32, (PAD, HEAD), 0)
    out = jnp.zeros((PAD, HEAD), jnp.float32)
    for number, row in enumerate(rows):
        out = jnp.where(which == number, jnp.broadcast_to(row, (PAD, HEAD)), out)
    return out.astype(jnp.bfloat16)


def summary_kernel(
    base_ref, lengths_hbm, q_hbm, g_hbm, decay_hbm, out_ref, q_buf, g_buf, decay_ref, lengths_ref, sems, small_sems
):
    rows = q_buf.shape[0]
    heads = decay_ref.shape[0]
    groups = sems.shape[1]
    width = q_buf.shape[1] // groups
    small = [
        pltpu.make_async_copy(lengths_hbm, lengths_ref, small_sems.at[0]),
        pltpu.make_async_copy(decay_hbm, decay_ref, small_sems.at[1]),
    ]
    for copy in small:
        copy.start()
    large = []
    for n in range(groups):
        span = slice(n * width, (n + 1) * width)
        pair = [
            pltpu.make_async_copy(q_hbm.at[:, span], q_buf.at[:, span], sems.at[0, n]),
            pltpu.make_async_copy(g_hbm.at[:, span], g_buf.at[:, span], sems.at[1, n]),
        ]
        for copy in pair:
            copy.start()
        large.append(pair)
    for copy in small:
        copy.wait()
    base = base_ref[0]
    by_row, cum = running_sums(decay_ref[...])
    before = scalar_segment(lengths_ref, base - 1)
    last = scalar_segment(lengths_ref, base + rows - 1)
    seg = token_segments(lengths_ref, base + lax.broadcasted_iota(jnp.int32, (rows, heads), 0))
    scale = jnp.where(seg == before, jnp.exp(cum), 0.0)
    factors = split3(jnp.where(last == before, jnp.exp(cum[rows - 1 : rows, :]), 0.0))
    for h in range(heads):
        cols = slice(h * HEAD, (h + 1) * HEAD)
        if (h * HEAD) % width == 0:
            for copy in large[h * HEAD // width]:
                copy.wait()
        scaled = q_buf[:, cols].astype(jnp.float32) * scale[:, h : h + 1]
        hi = scaled.astype(jnp.bfloat16)
        lo = (scaled - hi.astype(jnp.float32)).astype(jnp.bfloat16)
        g_t = g_buf[:, cols].T
        summary = jnp.dot(
            jnp.concatenate([g_t, g_t], axis=1),
            jnp.concatenate([hi, lo], axis=0),
            preferred_element_type=jnp.float32,
        )
        summary = summary.astype(jnp.bfloat16)
        extra = pad_rows([f[:, h : h + 1] for f in factors])
        for part in range(HEAD // HALF):
            slot = h * (HEAD // HALF) + part
            out_ref[slot, 0:HALF, :] = summary[part * HALF : (part + 1) * HALF, :]
            out_ref[slot, HALF : HALF + PAD, :] = extra


def inside_kernel(
    first, base_ref, lengths_ref, q_ref, k_ref, g_ref, decay_ref, after_ref, inside_ref, tail_ref, keys_ref
):
    rows = q_ref.shape[0]
    heads = decay_ref.shape[0]
    base = base_ref[0]
    cum_rows, cum = running_sums(decay_ref[...])
    last = scalar_segment(lengths_ref, base + rows - 1)
    seg = token_segments(lengths_ref, base + lax.broadcasted_iota(jnp.int32, (rows, heads), 0))
    tail_ref[...] = jnp.where(seg == last, jnp.exp(cum[rows - 1 : rows, :] - cum), 0.0)
    i_pos = lax.broadcasted_iota(jnp.int32, (rows, rows), 0)
    t_pos = lax.broadcasted_iota(jnp.int32, (rows, rows), 1)
    same = token_segments(lengths_ref, base + i_pos) == token_segments(lengths_ref, base + t_pos)
    bias = jnp.where(same & (t_pos >= i_pos), 0.0, NEG)
    for n in range(inside_ref.shape[1] // HEAD):
        h = first + n
        cols = slice(h * HEAD, (h + 1) * HEAD)
        here = slice(n * HEAD, (n + 1) * HEAD)
        keys = k_ref[:, cols]
        keys_ref[:, here] = keys
        scores = lax.dot_general(
            keys, q_ref[:, cols], (((1,), (1,)), ((), ())), preferred_element_type=jnp.float32
        )
        gaps = jnp.minimum(cum_rows[h : h + 1, :] - cum[:, h : h + 1], 0.0)
        weights = (jnp.exp(gaps + bias) * scores).astype(jnp.bfloat16)
        inside_ref[:, here] = jnp.dot(weights, g_ref[:, cols], preferred_element_type=jnp.float32)


def factor_row(ref, p):
    tail = ref[p, HALF : HALF + PAD, :].astype(jnp.float32)
    return tail[0:1, :] + tail[1:2, :] + tail[2:3, :]


def write_packet(ref, state, factor):
    size = jnp.abs(state)
    largest = jnp.max(jnp.max(size, axis=0, keepdims=True), axis=1, keepdims=True)
    bound = (largest * 1.01 + TINY).astype(jnp.bfloat16).astype(jnp.float32)
    code = jnp.exp2(size * ((2.0 * OCTAVES) / bound) - OCTAVES)
    ref[0:HALF, :] = jnp.where(state < 0.0, -code, code).astype(jnp.bfloat16)
    ref[HALF : HALF + PAD, :] = pad_rows([bound] + split3(factor))


def read_packet(ref):
    code = ref[0:HALF, :].astype(jnp.float32)
    tail = ref[HALF : HALF + PAD, :].astype(jnp.float32)
    octaves = jnp.log2(jnp.maximum(jnp.abs(code), 2.0**-OCTAVES)) + OCTAVES
    size = octaves * (tail[0:1, :] * (0.5 / OCTAVES))
    return jnp.where(code < 0.0, -size, size), tail[1:2, :] + tail[2:3, :] + tail[3:4, :]


def reduce_kernel(parts_ref, total_ref, factor_ref, packet_ref):
    state = jnp.zeros((HALF, HEAD), jnp.float32)
    factor = jnp.ones((1, HEAD), jnp.float32)
    for p in reversed(range(parts_ref.shape[0])):
        f = factor_row(parts_ref, p)
        state = parts_ref[p, 0:HALF, :].astype(jnp.float32) + f * state
        factor = factor * f
    total_ref[...] = state
    factor_ref[...] = factor
    write_packet(packet_ref, state, factor)


def join(refs):
    state, factor = read_packet(refs[-1])
    for ref in reversed(refs[:-1]):
        s, f = read_packet(ref)
        state = s + f * state
        factor = f * factor
    return state, factor


def join_kernel(after_ref, total_ref, factor_ref, *refs):
    near_ref, near_factor_ref, packet_ref = refs[-3:]
    state, factor = join(refs[:-3])
    near_ref[...] = state
    near_factor_ref[...] = factor
    own = factor_ref[...]
    write_packet(packet_ref, total_ref[...] + own * state, own * factor)


def states_kernel(after_ref, parts_ref, near_ref, near_factor_ref, *refs):
    out_ref = refs[-1]
    far, far_factor = join(refs[:-1])
    state = near_ref[...] + near_factor_ref[...] * far
    for p in reversed(range(parts_ref.shape[0])):
        out_ref[p] = state.astype(jnp.bfloat16)
        state = parts_ref[p, 0:HALF, :].astype(jnp.float32) + factor_row(parts_ref, p) * state


def output_kernel(tail_ref, states_ref, *refs):
    halves = refs[:-3]
    out_hbm, out_buf, sems = refs[-3:]
    groups = sems.shape[0]
    width = out_buf.shape[1] // groups
    tail = tail_ref[...]
    copies = []
    each = states_ref.shape[0] // (len(halves) // 2)
    for h in range(states_ref.shape[0]):
        keys_ref, inside_ref = halves[h // each * 2 : h // each * 2 + 2]
        cols = slice(h * HEAD, (h + 1) * HEAD)
        here = slice(h % each * HEAD, (h % each + 1) * HEAD)
        carried = lax.dot_general(
            keys_ref[:, here], states_ref[h], (((1,), (1,)), ((), ())), preferred_element_type=jnp.float32
        )
        out_buf[:, cols] = (inside_ref[:, here] + tail[:, h : h + 1] * carried).astype(jnp.bfloat16)
        if ((h + 1) * HEAD) % width == 0:
            n = h * HEAD // width
            span = slice(n * width, (n + 1) * width)
            copies.append(pltpu.make_async_copy(out_buf.at[:, span], out_hbm.at[:, span], sems.at[n]))
            copies[-1].start()
    for copy in copies:
        copy.wait()


SMEM = pl.BlockSpec(memory_space=pltpu.SMEM)
VMEM = pl.BlockSpec(memory_space=pltpu.VMEM)
REST = pl.BlockSpec(memory_space=pltpu.HBM)


def call(kernel, out_shape, in_specs, args, out_specs=None, scratch=()):
    if out_specs is None:
        out_specs = [VMEM] * len(out_shape) if isinstance(out_shape, (list, tuple)) else VMEM
    return pl.pallas_call(
        kernel,
        out_shape=out_shape,
        in_specs=in_specs,
        out_specs=out_specs,
        scratch_shapes=list(scratch),
        compiler_params=pltpu.CompilerParams(vmem_limit_bytes=40 * 1024 * 1024),
    )(*args)


def from_ahead(x, by):
    size = lax.axis_size("zh")
    return lax.ppermute(x, "zh", [(i + by, i) for i in range(size - by)])


def body(query_vectors, key_vectors, out_grad, log_decay, doc_lengths):
    rows, heads = log_decay.shape
    columns = query_vectors.shape[1]
    slots = columns // HALF
    index = lax.axis_index(("zh",) + GROUP)
    base = (index * rows).astype(jnp.int32).reshape(1)
    decay_rows = log_decay.T
    shape = jax.ShapeDtypeStruct
    dma = pltpu.SemaphoreType.DMA
    pinned = [
        pltpu.with_memory_space_constraint(x, pltpu.HBM) for x in (doc_lengths, query_vectors, out_grad, decay_rows)
    ]
    summaries = call(
        summary_kernel,
        shape((slots, HALF + PAD, HEAD), jnp.bfloat16),
        [SMEM] + [REST] * 4,
        (base, *pinned),
        scratch=(
            pltpu.VMEM((rows, columns), jnp.bfloat16),
            pltpu.VMEM((rows, columns), jnp.bfloat16),
            pltpu.VMEM((heads, rows), jnp.bfloat16),
            pltpu.SMEM(doc_lengths.shape, jnp.int32),
            dma((2, GROUPS)),
            dma((2,)),
        ),
    )
    parts = lax.all_to_all(summaries, GROUP, split_axis=0, concat_axis=0, tiled=True)
    state = shape((HALF, HEAD), jnp.float32)
    factor = shape((1, HEAD), jnp.float32)
    packet = shape((HALF + PAD, HEAD), jnp.bfloat16)
    total, total_factor, own = call(reduce_kernel, (state, factor, packet), [VMEM], (parts,))

    def inside_part(number, after):
        return call(
            functools.partial(inside_kernel, number * heads // 2),
            (
                shape((rows, columns // 2), jnp.float32),
                shape((rows, heads), jnp.float32),
                shape((rows, columns // 2), jnp.bfloat16),
            ),
            [SMEM] * 2 + [VMEM] * 5,
            (base, doc_lengths, query_vectors, key_vectors, out_grad, decay_rows, after),
        )

    ahead = [from_ahead(own, by) for by in (1, 2)]
    inside_a, tail, keys_a = inside_part(0, own)
    near, near_factor, wide = call(
        join_kernel, (state, factor, packet), [VMEM] * 5, (tail, total, total_factor, *ahead)
    )
    far = [from_ahead(wide, by) for by in (3, 6)]
    inside_b, tail_b, keys_b = inside_part(1, wide)
    states = call(
        states_kernel,
        shape((slots, HALF, HEAD), jnp.bfloat16),
        [VMEM] * 6,
        (tail_b, parts, near, near_factor, *far),
    )
    mine = lax.all_to_all(states, GROUP, split_axis=0, concat_axis=0, tiled=True)
    mine = mine.reshape(heads, HEAD, HEAD)
    return call(
        output_kernel,
        shape((rows, columns), jnp.bfloat16),
        [VMEM] * 6,
        (tail, mine, keys_a, inside_a, keys_b, inside_b),
        out_specs=REST,
        scratch=(pltpu.VMEM((rows, columns), jnp.bfloat16), dma((GROUPS,))),
    )


def solution(mesh):
    side = 4
    fine = Mesh(
        mesh.devices.reshape(mesh.shape["seq"] // 4, 2, 2, side, mesh.shape["head"] // side), ("zh",) + GROUP
    )
    tokens = P(("zh",) + GROUP, None)
    return jax.shard_map(
        body, mesh=fine, in_specs=(tokens, tokens, tokens, tokens, P()), out_specs=tokens, check_vma=False
    )
```

```python
import functools
import jax
import jax.numpy as jnp
from jax import lax
from jax.experimental import pallas as pl
from jax.experimental.pallas import tpu as pltpu
from jax.sharding import Mesh, PartitionSpec as P

HEAD = 128
PAD = 8
HALF = 64
RADICES = (2, 4)
ORDERS = ((1,), (2, 6, 4))
ROW_PARTS = 1
NEG = -1e30
TINY = 1e-36
OCTAVES = 120.0
GROUPS = 2
GROUP = ("zl", "core", "x", "y")


def token_segments(lengths_ref, positions):
    start = jnp.int32(0)
    total = jnp.zeros(positions.shape, jnp.int32)
    for d in range(lengths_ref.shape[0]):
        total = total + (start <= positions).astype(jnp.int32)
        start = start + lengths_ref[d]
    return total


def scalar_segment(lengths_ref, position):
    start = jnp.int32(0)
    total = jnp.int32(0)
    for d in range(lengths_ref.shape[0]):
        total = total + (start <= position).astype(jnp.int32)
        start = start + lengths_ref[d]
    return total


def running_sums(decay_rows):
    size = decay_rows.shape[1]
    upto = lax.broadcasted_iota(jnp.int32, (size, size), 0) <= lax.broadcasted_iota(jnp.int32, (size, size), 1)
    by_row = jnp.dot(decay_rows, upto.astype(jnp.bfloat16), preferred_element_type=jnp.float32)
    since = lax.broadcasted_iota(jnp.int32, (size, size), 0) >= lax.broadcasted_iota(jnp.int32, (size, size), 1)
    by_col = lax.dot_general(
        since.astype(jnp.bfloat16), decay_rows, (((1,), (1,)), ((), ())), preferred_element_type=jnp.float32
    )
    return by_row, by_col


def split3(value):
    hi = value.astype(jnp.bfloat16)
    rest = value - hi.astype(jnp.float32)
    mid = rest.astype(jnp.bfloat16)
    lo = (rest - mid.astype(jnp.float32)).astype(jnp.bfloat16)
    return [part.astype(jnp.float32) for part in (hi, mid, lo)]


def pad_rows(rows):
    which = lax.broadcasted_iota(jnp.int32, (PAD, HEAD), 0)
    out = jnp.zeros((PAD, HEAD), jnp.float32)
    for number, row in enumerate(rows):
        out = jnp.where(which == number, jnp.broadcast_to(row, (PAD, HEAD)), out)
    return out.astype(jnp.bfloat16)


def summary_kernel(
    base_ref, lengths_hbm, q_hbm, g_hbm, decay_hbm, out_ref, q_buf, g_buf, decay_ref, lengths_ref, sems, small_sems
):
    rows = q_buf.shape[0]
    heads = decay_ref.shape[0]
    groups = sems.shape[1] // ROW_PARTS
    width = q_buf.shape[1] // groups
    small = [
        pltpu.make_async_copy(lengths_hbm, lengths_ref, small_sems.at[0]),
        pltpu.make_async_copy(decay_hbm, decay_ref, small_sems.at[1]),
    ]
    for copy in small:
        copy.start()
    large = []
    for n in range(groups):
        span = slice(n * width, (n + 1) * width)
        pair = []
        for r in range(ROW_PARTS):
            band = slice(r * rows // ROW_PARTS, (r + 1) * rows // ROW_PARTS)
            pair += [
                pltpu.make_async_copy(q_hbm.at[band, span], q_buf.at[band, span], sems.at[0, n * ROW_PARTS + r]),
                pltpu.make_async_copy(g_hbm.at[band, span], g_buf.at[band, span], sems.at[1, n * ROW_PARTS + r]),
            ]
        for copy in pair:
            copy.start()
        large.append(pair)
    for copy in small:
        copy.wait()
    base = base_ref[0]
    by_row, cum = running_sums(decay_ref[...])
    before = scalar_segment(lengths_ref, base - 1)
    last = scalar_segment(lengths_ref, base + rows - 1)
    seg = token_segments(lengths_ref, base + lax.broadcasted_iota(jnp.int32, (rows, heads), 0))
    scale = jnp.where(seg == before, jnp.exp(cum), 0.0)
    factors = split3(jnp.where(last == before, jnp.exp(cum[rows - 1 : rows, :]), 0.0))
    for h in range(heads):
        cols = slice(h * HEAD, (h + 1) * HEAD)
        if (h * HEAD) % width == 0:
            for copy in large[h * HEAD // width]:
                copy.wait()
        scaled = q_buf[:, cols].astype(jnp.float32) * scale[:, h : h + 1]
        hi = scaled.astype(jnp.bfloat16)
        lo = (scaled - hi.astype(jnp.float32)).astype(jnp.bfloat16)
        g_t = g_buf[:, cols].T
        summary = jnp.dot(
            jnp.concatenate([g_t, g_t], axis=1),
            jnp.concatenate([hi, lo], axis=0),
            preferred_element_type=jnp.float32,
        )
        summary = summary.astype(jnp.bfloat16)
        extra = pad_rows([f[:, h : h + 1] for f in factors])
        for part in range(HEAD // HALF):
            slot = h * (HEAD // HALF) + part
            out_ref[slot, 0:HALF, :] = summary[part * HALF : (part + 1) * HALF, :]
            out_ref[slot, HALF : HALF + PAD, :] = extra


def inside_kernel(
    first, base_ref, lengths_ref, q_ref, k_ref, g_ref, decay_ref, after_ref, inside_ref, tail_ref, keys_ref
):
    rows = q_ref.shape[0]
    heads = decay_ref.shape[0]
    base = base_ref[0]
    cum_rows, cum = running_sums(decay_ref[...])
    last = scalar_segment(lengths_ref, base + rows - 1)
    seg = token_segments(lengths_ref, base + lax.broadcasted_iota(jnp.int32, (rows, heads), 0))
    tail_ref[...] = jnp.where(seg == last, jnp.exp(cum[rows - 1 : rows, :] - cum), 0.0)
    i_pos = lax.broadcasted_iota(jnp.int32, (rows, rows), 0)
    t_pos = lax.broadcasted_iota(jnp.int32, (rows, rows), 1)
    same = token_segments(lengths_ref, base + i_pos) == token_segments(lengths_ref, base + t_pos)
    bias = jnp.where(same & (t_pos >= i_pos), 0.0, NEG)
    for n in range(inside_ref.shape[1] // HEAD):
        h = first + n
        cols = slice(h * HEAD, (h + 1) * HEAD)
        here = slice(n * HEAD, (n + 1) * HEAD)
        keys = k_ref[:, cols]
        keys_ref[:, here] = keys
        scores = lax.dot_general(
            keys, q_ref[:, cols], (((1,), (1,)), ((), ())), preferred_element_type=jnp.float32
        )
        gaps = jnp.minimum(cum_rows[h : h + 1, :] - cum[:, h : h + 1], 0.0)
        weights = (jnp.exp(gaps + bias) * scores).astype(jnp.bfloat16)
        inside_ref[:, here] = jnp.dot(weights, g_ref[:, cols], preferred_element_type=jnp.float32)


def factor_row(ref, p):
    tail = ref[p, HALF : HALF + PAD, :].astype(jnp.float32)
    return tail[0:1, :] + tail[1:2, :] + tail[2:3, :]


def write_packet(ref, state, factor):
    size = jnp.abs(state)
    largest = jnp.max(jnp.max(size, axis=0, keepdims=True), axis=1, keepdims=True)
    bound = (largest * 1.01 + TINY).astype(jnp.bfloat16).astype(jnp.float32)
    code = jnp.exp2(size * ((2.0 * OCTAVES) / bound) - OCTAVES)
    ref[0:HALF, :] = jnp.where(state < 0.0, -code, code).astype(jnp.bfloat16)
    ref[HALF : HALF + PAD, :] = pad_rows([bound] + split3(factor))


def read_packet(ref):
    code = ref[0:HALF, :].astype(jnp.float32)
    tail = ref[HALF : HALF + PAD, :].astype(jnp.float32)
    octaves = jnp.log2(jnp.maximum(jnp.abs(code), 2.0**-OCTAVES)) + OCTAVES
    size = octaves * (tail[0:1, :] * (0.5 / OCTAVES))
    return jnp.where(code < 0.0, -size, size), tail[1:2, :] + tail[2:3, :] + tail[3:4, :]


def reduce_kernel(parts_ref, total_ref, factor_ref, packet_ref):
    state = jnp.zeros((HALF, HEAD), jnp.float32)
    factor = jnp.ones((1, HEAD), jnp.float32)
    for p in reversed(range(parts_ref.shape[0])):
        f = factor_row(parts_ref, p)
        state = parts_ref[p, 0:HALF, :].astype(jnp.float32) + f * state
        factor = factor * f
    total_ref[...] = state
    factor_ref[...] = factor
    write_packet(packet_ref, state, factor)


def join(shifts, refs):
    state = jnp.zeros((HALF, HEAD), jnp.float32)
    factor = jnp.ones((1, HEAD), jnp.float32)
    for by, ref in sorted(zip(shifts, refs), key=lambda item: -item[0]):
        s, f = read_packet(ref)
        state = s + f * state
        factor = f * factor
    return state, factor


def join_kernel(shifts, after_ref, total_ref, factor_ref, *refs):
    refs, outs = refs[:-3], refs[-3:]
    near_ref, near_factor_ref, packet_ref = outs
    state, factor = join(shifts, refs[-len(shifts) :])
    if len(refs) > len(shifts):
        state = refs[0][...] + refs[1][...] * state
        factor = refs[1][...] * factor
    near_ref[...] = state
    near_factor_ref[...] = factor
    own = factor_ref[...]
    write_packet(packet_ref, total_ref[...] + own * state, own * factor)


def states_kernel(shifts, after_ref, parts_ref, near_ref, near_factor_ref, *refs):
    out_ref = refs[-1]
    far, far_factor = join(shifts, refs[:-1])
    state = near_ref[...] + near_factor_ref[...] * far
    for p in reversed(range(parts_ref.shape[0])):
        out_ref[p] = state.astype(jnp.bfloat16)
        state = parts_ref[p, 0:HALF, :].astype(jnp.float32) + factor_row(parts_ref, p) * state


def output_kernel(pieces, tail_ref, states_ref, *refs):
    parts = refs[:-3]
    out_hbm, out_buf, sems = refs[-3:]
    owner = [(n, h - first) for n, (first, count) in enumerate(pieces) for h in range(first, first + count)]
    groups = sems.shape[0]
    width = out_buf.shape[1] // groups
    tail = tail_ref[...]
    copies = []
    for h in range(states_ref.shape[0]):
        n, place = owner[h]
        keys_ref, inside_ref = parts[2 * n : 2 * n + 2]
        cols = slice(h * HEAD, (h + 1) * HEAD)
        here = slice(place * HEAD, (place + 1) * HEAD)
        carried = lax.dot_general(
            keys_ref[:, here], states_ref[h], (((1,), (1,)), ((), ())), preferred_element_type=jnp.float32
        )
        out_buf[:, cols] = (inside_ref[:, here] + tail[:, h : h + 1] * carried).astype(jnp.bfloat16)
        if ((h + 1) * HEAD) % width == 0:
            n = h * HEAD // width
            span = slice(n * width, (n + 1) * width)
            copies.append(pltpu.make_async_copy(out_buf.at[:, span], out_hbm.at[:, span], sems.at[n]))
            copies[-1].start()
    for copy in copies:
        copy.wait()


SMEM = pl.BlockSpec(memory_space=pltpu.SMEM)
VMEM = pl.BlockSpec(memory_space=pltpu.VMEM)
REST = pl.BlockSpec(memory_space=pltpu.HBM)


def call(kernel, out_shape, in_specs, args, out_specs=None, scratch=()):
    if out_specs is None:
        out_specs = [VMEM] * len(out_shape) if isinstance(out_shape, (list, tuple)) else VMEM
    return pl.pallas_call(
        kernel,
        out_shape=out_shape,
        in_specs=in_specs,
        out_specs=out_specs,
        scratch_shapes=list(scratch),
        compiler_params=pltpu.CompilerParams(vmem_limit_bytes=40 * 1024 * 1024),
    )(*args)


def from_ahead(x, by):
    size = lax.axis_size("zh")
    return lax.ppermute(x, "zh", [(i + by, i) for i in range(size - by)])


def body(query_vectors, key_vectors, out_grad, log_decay, doc_lengths):
    rows, heads = log_decay.shape
    columns = query_vectors.shape[1]
    slots = columns // HALF
    index = lax.axis_index(("zh",) + GROUP)
    base = (index * rows).astype(jnp.int32).reshape(1)
    decay_rows = log_decay.T
    shape = jax.ShapeDtypeStruct
    dma = pltpu.SemaphoreType.DMA
    pinned = [
        pltpu.with_memory_space_constraint(x, pltpu.HBM) for x in (doc_lengths, query_vectors, out_grad, decay_rows)
    ]
    summaries = call(
        summary_kernel,
        shape((slots, HALF + PAD, HEAD), jnp.bfloat16),
        [SMEM] + [REST] * 4,
        (base, *pinned),
        scratch=(
            pltpu.VMEM((rows, columns), jnp.bfloat16),
            pltpu.VMEM((rows, columns), jnp.bfloat16),
            pltpu.VMEM((heads, rows), jnp.bfloat16),
            pltpu.SMEM(doc_lengths.shape, jnp.int32),
            dma((2, GROUPS * ROW_PARTS)),
            dma((2,)),
        ),
    )
    parts = lax.all_to_all(summaries, GROUP, split_axis=0, concat_axis=0, tiled=True)
    state = shape((HALF, HEAD), jnp.float32)
    factor = shape((1, HEAD), jnp.float32)
    packet = shape((HALF + PAD, HEAD), jnp.bfloat16)
    total, total_factor, own = call(reduce_kernel, (state, factor, packet), [VMEM], (parts,))

    count = len(RADICES)
    edges = [heads * n // count for n in range(count + 1)]
    pieces = tuple((edges[n], edges[n + 1] - edges[n]) for n in range(count))

    def inside_part(number, after):
        first, here = pieces[number]
        return call(
            functools.partial(inside_kernel, first),
            (
                shape((rows, here * HEAD), jnp.float32),
                shape((rows, heads), jnp.float32),
                shape((rows, here * HEAD), jnp.bfloat16),
            ),
            [SMEM] * 2 + [VMEM] * 5,
            (base, doc_lengths, query_vectors, key_vectors, out_grad, decay_rows, after),
        )

    step = 1
    near = ()
    done = []
    for number, radix in enumerate(RADICES):
        shifts = ORDERS[number]
        ahead = [from_ahead(own, by) for by in shifts]
        inside, tail, keys = inside_part(number, own)
        done += [keys, inside]
        step *= radix
        if number + 1 < count:
            *near, own = call(
                functools.partial(join_kernel, shifts),
                (state, factor, packet),
                [VMEM] * (3 + len(near) + len(ahead)),
                (tail, total, total_factor, *near, *ahead),
            )
    states = call(
        functools.partial(states_kernel, shifts),
        shape((slots, HALF, HEAD), jnp.bfloat16),
        [VMEM] * (4 + len(ahead)),
        (tail, parts, *near, *ahead),
    )
    mine = lax.all_to_all(states, GROUP, split_axis=0, concat_axis=0, tiled=True)
    mine = mine.reshape(heads, HEAD, HEAD)
    return call(
        functools.partial(output_kernel, pieces),
        shape((rows, columns), jnp.bfloat16),
        [VMEM] * (2 + len(done)),
        (tail, mine, *done),
        out_specs=REST,
        scratch=(pltpu.VMEM((rows, columns), jnp.bfloat16), dma((GROUPS,))),
    )


def solution(mesh):
    side = 4
    fine = Mesh(
        mesh.devices.reshape(mesh.shape["seq"] // 4, 2, 2, side, mesh.shape["head"] // side), ("zh",) + GROUP
    )
    tokens = P(("zh",) + GROUP, None)
    return jax.shard_map(
        body, mesh=fine, in_specs=(tokens, tokens, tokens, tokens, P()), out_specs=tokens, check_vma=False
    )
```

```python
import functools
import jax
import jax.numpy as jnp
from jax import lax
from jax.experimental import pallas as pl
from jax.experimental.pallas import tpu as pltpu
from jax.sharding import Mesh, PartitionSpec as P

HEAD = 128
PAD = 8
HALF = 64
FIRST = (1, 4, 5)
SECOND = (2, 6)
ROW_PARTS = 1
NEG = -1e30
TINY = 1e-36
OCTAVES = 120.0
GROUPS = 2
GROUP = ("zl", "core", "x", "y")


def token_segments(lengths_ref, positions):
    start = jnp.int32(0)
    total = jnp.zeros(positions.shape, jnp.int32)
    for d in range(lengths_ref.shape[0]):
        total = total + (start <= positions).astype(jnp.int32)
        start = start + lengths_ref[d]
    return total


def scalar_segment(lengths_ref, position):
    start = jnp.int32(0)
    total = jnp.int32(0)
    for d in range(lengths_ref.shape[0]):
        total = total + (start <= position).astype(jnp.int32)
        start = start + lengths_ref[d]
    return total


def running_sums(decay_rows):
    size = decay_rows.shape[1]
    upto = lax.broadcasted_iota(jnp.int32, (size, size), 0) <= lax.broadcasted_iota(jnp.int32, (size, size), 1)
    by_row = jnp.dot(decay_rows, upto.astype(jnp.bfloat16), preferred_element_type=jnp.float32)
    since = lax.broadcasted_iota(jnp.int32, (size, size), 0) >= lax.broadcasted_iota(jnp.int32, (size, size), 1)
    by_col = lax.dot_general(
        since.astype(jnp.bfloat16), decay_rows, (((1,), (1,)), ((), ())), preferred_element_type=jnp.float32
    )
    return by_row, by_col


def split3(value):
    hi = value.astype(jnp.bfloat16)
    rest = value - hi.astype(jnp.float32)
    mid = rest.astype(jnp.bfloat16)
    lo = (rest - mid.astype(jnp.float32)).astype(jnp.bfloat16)
    return [part.astype(jnp.float32) for part in (hi, mid, lo)]


def pad_rows(rows):
    which = lax.broadcasted_iota(jnp.int32, (PAD, HEAD), 0)
    out = jnp.zeros((PAD, HEAD), jnp.float32)
    for number, row in enumerate(rows):
        out = jnp.where(which == number, jnp.broadcast_to(row, (PAD, HEAD)), out)
    return out.astype(jnp.bfloat16)


def summary_kernel(
    base_ref, lengths_hbm, q_hbm, g_hbm, decay_hbm, out_ref, q_buf, g_buf, decay_ref, lengths_ref, sems, small_sems
):
    rows = q_buf.shape[0]
    heads = decay_ref.shape[0]
    groups = sems.shape[1] // ROW_PARTS
    width = q_buf.shape[1] // groups
    small = [
        pltpu.make_async_copy(lengths_hbm, lengths_ref, small_sems.at[0]),
        pltpu.make_async_copy(decay_hbm, decay_ref, small_sems.at[1]),
    ]
    for copy in small:
        copy.start()
    large = []
    for n in range(groups):
        span = slice(n * width, (n + 1) * width)
        pair = []
        for r in range(ROW_PARTS):
            band = slice(r * rows // ROW_PARTS, (r + 1) * rows // ROW_PARTS)
            pair += [
                pltpu.make_async_copy(q_hbm.at[band, span], q_buf.at[band, span], sems.at[0, n * ROW_PARTS + r]),
                pltpu.make_async_copy(g_hbm.at[band, span], g_buf.at[band, span], sems.at[1, n * ROW_PARTS + r]),
            ]
        for copy in pair:
            copy.start()
        large.append(pair)
    for copy in small:
        copy.wait()
    base = base_ref[0]
    by_row, cum = running_sums(decay_ref[...])
    before = scalar_segment(lengths_ref, base - 1)
    last = scalar_segment(lengths_ref, base + rows - 1)
    seg = token_segments(lengths_ref, base + lax.broadcasted_iota(jnp.int32, (rows, heads), 0))
    scale = jnp.where(seg == before, jnp.exp(cum), 0.0)
    factors = split3(jnp.where(last == before, jnp.exp(cum[rows - 1 : rows, :]), 0.0))
    for h in range(heads):
        cols = slice(h * HEAD, (h + 1) * HEAD)
        if (h * HEAD) % width == 0:
            for copy in large[h * HEAD // width]:
                copy.wait()
        scaled = q_buf[:, cols].astype(jnp.float32) * scale[:, h : h + 1]
        hi = scaled.astype(jnp.bfloat16)
        lo = (scaled - hi.astype(jnp.float32)).astype(jnp.bfloat16)
        g_t = g_buf[:, cols].T
        summary = jnp.dot(
            jnp.concatenate([g_t, g_t], axis=1),
            jnp.concatenate([hi, lo], axis=0),
            preferred_element_type=jnp.float32,
        )
        summary = summary.astype(jnp.bfloat16)
        extra = pad_rows([f[:, h : h + 1] for f in factors])
        for part in range(HEAD // HALF):
            slot = h * (HEAD // HALF) + part
            out_ref[slot, 0:HALF, :] = summary[part * HALF : (part + 1) * HALF, :]
            out_ref[slot, HALF : HALF + PAD, :] = extra


def inside_kernel(
    first, base_ref, lengths_ref, q_ref, k_ref, g_ref, decay_ref, after_ref, inside_ref, tail_ref, keys_ref
):
    rows = q_ref.shape[0]
    heads = decay_ref.shape[0]
    base = base_ref[0]
    cum_rows, cum = running_sums(decay_ref[...])
    last = scalar_segment(lengths_ref, base + rows - 1)
    seg = token_segments(lengths_ref, base + lax.broadcasted_iota(jnp.int32, (rows, heads), 0))
    tail_ref[...] = jnp.where(seg == last, jnp.exp(cum[rows - 1 : rows, :] - cum), 0.0)
    i_pos = lax.broadcasted_iota(jnp.int32, (rows, rows), 0)
    t_pos = lax.broadcasted_iota(jnp.int32, (rows, rows), 1)
    same = token_segments(lengths_ref, base + i_pos) == token_segments(lengths_ref, base + t_pos)
    bias = jnp.where(same & (t_pos >= i_pos), 0.0, NEG)
    for n in range(inside_ref.shape[1] // HEAD):
        h = first + n
        cols = slice(h * HEAD, (h + 1) * HEAD)
        here = slice(n * HEAD, (n + 1) * HEAD)
        keys = k_ref[:, cols]
        keys_ref[:, here] = keys
        scores = lax.dot_general(
            keys, q_ref[:, cols], (((1,), (1,)), ((), ())), preferred_element_type=jnp.float32
        )
        gaps = jnp.minimum(cum_rows[h : h + 1, :] - cum[:, h : h + 1], 0.0)
        weights = (jnp.exp(gaps + bias) * scores).astype(jnp.bfloat16)
        inside_ref[:, here] = jnp.dot(weights, g_ref[:, cols], preferred_element_type=jnp.float32)


def factor_row(ref, p):
    tail = ref[p, HALF : HALF + PAD, :].astype(jnp.float32)
    return tail[0:1, :] + tail[1:2, :] + tail[2:3, :]


def write_packet(ref, state, factor):
    size = jnp.abs(state)
    largest = jnp.max(jnp.max(size, axis=0, keepdims=True), axis=1, keepdims=True)
    bound = (largest * 1.01 + TINY).astype(jnp.bfloat16).astype(jnp.float32)
    code = jnp.exp2(size * ((2.0 * OCTAVES) / bound) - OCTAVES)
    ref[0:HALF, :] = jnp.where(state < 0.0, -code, code).astype(jnp.bfloat16)
    ref[HALF : HALF + PAD, :] = pad_rows([bound] + split3(factor))


def read_packet(ref):
    code = ref[0:HALF, :].astype(jnp.float32)
    tail = ref[HALF : HALF + PAD, :].astype(jnp.float32)
    octaves = jnp.log2(jnp.maximum(jnp.abs(code), 2.0**-OCTAVES)) + OCTAVES
    size = octaves * (tail[0:1, :] * (0.5 / OCTAVES))
    return jnp.where(code < 0.0, -size, size), tail[1:2, :] + tail[2:3, :] + tail[3:4, :]


def reduce_kernel(parts_ref, total_ref, factor_ref, packet_ref):
    state = jnp.zeros((HALF, HEAD), jnp.float32)
    factor = jnp.ones((1, HEAD), jnp.float32)
    for p in reversed(range(parts_ref.shape[0])):
        f = factor_row(parts_ref, p)
        state = parts_ref[p, 0:HALF, :].astype(jnp.float32) + f * state
        factor = factor * f
    total_ref[...] = state
    factor_ref[...] = factor
    write_packet(packet_ref, state, factor)


def join(shifts, refs):
    state = jnp.zeros((HALF, HEAD), jnp.float32)
    factor = jnp.ones((1, HEAD), jnp.float32)
    for by, ref in sorted(zip(shifts, refs), key=lambda item: -item[0]):
        s, f = read_packet(ref)
        state = s + f * state
        factor = f * factor
    return state, factor


def join_kernel(total_ref, factor_ref, next_ref, near_ref, near_factor_ref, packet_ref):
    state, factor = read_packet(next_ref)
    near_ref[...] = state
    near_factor_ref[...] = factor
    own = factor_ref[...]
    write_packet(packet_ref, total_ref[...] + own * state, own * factor)


def states_kernel(shifts, after_ref, parts_ref, near_ref, near_factor_ref, *refs):
    out_ref = refs[-1]
    far, far_factor = join(shifts, refs[:-1])
    state = near_ref[...] + near_factor_ref[...] * far
    for p in reversed(range(parts_ref.shape[0])):
        out_ref[p] = state.astype(jnp.bfloat16)
        state = parts_ref[p, 0:HALF, :].astype(jnp.float32) + factor_row(parts_ref, p) * state


def output_kernel(pieces, tail_ref, states_ref, *refs):
    parts = refs[:-3]
    out_hbm, out_buf, sems = refs[-3:]
    owner = [(n, h - first) for n, (first, count) in enumerate(pieces) for h in range(first, first + count)]
    groups = sems.shape[0]
    width = out_buf.shape[1] // groups
    tail = tail_ref[...]
    copies = []
    for h in range(states_ref.shape[0]):
        n, place = owner[h]
        keys_ref, inside_ref = parts[2 * n : 2 * n + 2]
        cols = slice(h * HEAD, (h + 1) * HEAD)
        here = slice(place * HEAD, (place + 1) * HEAD)
        carried = lax.dot_general(
            keys_ref[:, here], states_ref[h], (((1,), (1,)), ((), ())), preferred_element_type=jnp.float32
        )
        out_buf[:, cols] = (inside_ref[:, here] + tail[:, h : h + 1] * carried).astype(jnp.bfloat16)
        if ((h + 1) * HEAD) % width == 0:
            n = h * HEAD // width
            span = slice(n * width, (n + 1) * width)
            copies.append(pltpu.make_async_copy(out_buf.at[:, span], out_hbm.at[:, span], sems.at[n]))
            copies[-1].start()
    for copy in copies:
        copy.wait()


SMEM = pl.BlockSpec(memory_space=pltpu.SMEM)
VMEM = pl.BlockSpec(memory_space=pltpu.VMEM)
REST = pl.BlockSpec(memory_space=pltpu.HBM)


def call(kernel, out_shape, in_specs, args, out_specs=None, scratch=()):
    if out_specs is None:
        out_specs = [VMEM] * len(out_shape) if isinstance(out_shape, (list, tuple)) else VMEM
    return pl.pallas_call(
        kernel,
        out_shape=out_shape,
        in_specs=in_specs,
        out_specs=out_specs,
        scratch_shapes=list(scratch),
        compiler_params=pltpu.CompilerParams(vmem_limit_bytes=40 * 1024 * 1024),
    )(*args)


def from_ahead(x, by):
    size = lax.axis_size("zh")
    return lax.ppermute(x, "zh", [(i + by, i) for i in range(size - by)])


def body(query_vectors, key_vectors, out_grad, log_decay, doc_lengths):
    rows, heads = log_decay.shape
    columns = query_vectors.shape[1]
    slots = columns // HALF
    index = lax.axis_index(("zh",) + GROUP)
    base = (index * rows).astype(jnp.int32).reshape(1)
    decay_rows = log_decay.T
    shape = jax.ShapeDtypeStruct
    dma = pltpu.SemaphoreType.DMA
    pinned = [
        pltpu.with_memory_space_constraint(x, pltpu.HBM) for x in (doc_lengths, query_vectors, out_grad, decay_rows)
    ]
    summaries = call(
        summary_kernel,
        shape((slots, HALF + PAD, HEAD), jnp.bfloat16),
        [SMEM] + [REST] * 4,
        (base, *pinned),
        scratch=(
            pltpu.VMEM((rows, columns), jnp.bfloat16),
            pltpu.VMEM((rows, columns), jnp.bfloat16),
            pltpu.VMEM((heads, rows), jnp.bfloat16),
            pltpu.SMEM(doc_lengths.shape, jnp.int32),
            dma((2, GROUPS * ROW_PARTS)),
            dma((2,)),
        ),
    )
    parts = lax.all_to_all(summaries, GROUP, split_axis=0, concat_axis=0, tiled=True)
    state = shape((HALF, HEAD), jnp.float32)
    factor = shape((1, HEAD), jnp.float32)
    packet = shape((HALF + PAD, HEAD), jnp.bfloat16)
    total, total_factor, own = call(reduce_kernel, (state, factor, packet), [VMEM], (parts,))

    count = 1
    edges = [heads * n // count for n in range(count + 1)]
    pieces = tuple((edges[n], edges[n + 1] - edges[n]) for n in range(count))

    def inside_part(number, after):
        first, here = pieces[number]
        return call(
            functools.partial(inside_kernel, first),
            (
                shape((rows, here * HEAD), jnp.float32),
                shape((rows, heads), jnp.float32),
                shape((rows, here * HEAD), jnp.bfloat16),
            ),
            [SMEM] * 2 + [VMEM] * 5,
            (base, doc_lengths, query_vectors, key_vectors, out_grad, decay_rows, after),
        )

    ahead = {by: from_ahead(own, by) for by in FIRST}
    near, near_factor, wide = call(
        join_kernel, (state, factor, packet), [VMEM] * 3, (total, total_factor, ahead.pop(1))
    )
    ahead.update({by: from_ahead(wide, by) for by in SECOND})
    inside, tail, keys = inside_part(0, wide)
    done = [keys, inside]
    shifts = tuple(sorted(ahead))
    states = call(
        functools.partial(states_kernel, shifts),
        shape((slots, HALF, HEAD), jnp.bfloat16),
        [VMEM] * (4 + len(shifts)),
        (tail, parts, near, near_factor, *[ahead[by] for by in shifts]),
    )
    mine = lax.all_to_all(states, GROUP, split_axis=0, concat_axis=0, tiled=True)
    mine = mine.reshape(heads, HEAD, HEAD)
    return call(
        functools.partial(output_kernel, pieces),
        shape((rows, columns), jnp.bfloat16),
        [VMEM] * (2 + len(done)),
        (tail, mine, *done),
        out_specs=REST,
        scratch=(pltpu.VMEM((rows, columns), jnp.bfloat16), dma((GROUPS,))),
    )


def solution(mesh):
    side = 4
    fine = Mesh(
        mesh.devices.reshape(mesh.shape["seq"] // 4, 2, 2, side, mesh.shape["head"] // side), ("zh",) + GROUP
    )
    tokens = P(("zh",) + GROUP, None)
    return jax.shard_map(
        body, mesh=fine, in_specs=(tokens, tokens, tokens, tokens, P()), out_specs=tokens, check_vma=False
    )
```

```python
import functools
import jax
import jax.numpy as jnp
from jax import lax
from jax.experimental import pallas as pl
from jax.experimental.pallas import tpu as pltpu
from jax.sharding import Mesh, PartitionSpec as P

HEAD = 128
PAD = 8
HALF = 64
FIRST = (1, 4, 5, 6, 7)
SECOND = (2,)
ROW_PARTS = 1
NEG = -1e30
TINY = 1e-36
OCTAVES = 120.0
GROUPS = 2
GROUP = ("zl", "core", "x", "y")


def token_segments(lengths_ref, positions):
    start = jnp.int32(0)
    total = jnp.zeros(positions.shape, jnp.int32)
    for d in range(lengths_ref.shape[0]):
        total = total + (start <= positions).astype(jnp.int32)
        start = start + lengths_ref[d]
    return total


def scalar_segment(lengths_ref, position):
    start = jnp.int32(0)
    total = jnp.int32(0)
    for d in range(lengths_ref.shape[0]):
        total = total + (start <= position).astype(jnp.int32)
        start = start + lengths_ref[d]
    return total


def running_sums(decay_rows):
    size = decay_rows.shape[1]
    upto = lax.broadcasted_iota(jnp.int32, (size, size), 0) <= lax.broadcasted_iota(jnp.int32, (size, size), 1)
    by_row = jnp.dot(decay_rows, upto.astype(jnp.bfloat16), preferred_element_type=jnp.float32)
    since = lax.broadcasted_iota(jnp.int32, (size, size), 0) >= lax.broadcasted_iota(jnp.int32, (size, size), 1)
    by_col = lax.dot_general(
        since.astype(jnp.bfloat16), decay_rows, (((1,), (1,)), ((), ())), preferred_element_type=jnp.float32
    )
    return by_row, by_col


def split3(value):
    hi = value.astype(jnp.bfloat16)
    rest = value - hi.astype(jnp.float32)
    mid = rest.astype(jnp.bfloat16)
    lo = (rest - mid.astype(jnp.float32)).astype(jnp.bfloat16)
    return [part.astype(jnp.float32) for part in (hi, mid, lo)]


def pad_rows(rows):
    which = lax.broadcasted_iota(jnp.int32, (PAD, HEAD), 0)
    out = jnp.zeros((PAD, HEAD), jnp.float32)
    for number, row in enumerate(rows):
        out = jnp.where(which == number, jnp.broadcast_to(row, (PAD, HEAD)), out)
    return out.astype(jnp.bfloat16)


def summary_kernel(
    base_ref, lengths_hbm, q_hbm, g_hbm, decay_hbm, out_ref, q_buf, g_buf, decay_ref, lengths_ref, sems, small_sems
):
    rows = q_buf.shape[0]
    heads = decay_ref.shape[0]
    groups = sems.shape[1] // ROW_PARTS
    width = q_buf.shape[1] // groups
    small = [
        pltpu.make_async_copy(lengths_hbm, lengths_ref, small_sems.at[0]),
        pltpu.make_async_copy(decay_hbm, decay_ref, small_sems.at[1]),
    ]
    for copy in small:
        copy.start()
    large = []
    for n in range(groups):
        span = slice(n * width, (n + 1) * width)
        pair = []
        for r in range(ROW_PARTS):
            band = slice(r * rows // ROW_PARTS, (r + 1) * rows // ROW_PARTS)
            pair += [
                pltpu.make_async_copy(q_hbm.at[band, span], q_buf.at[band, span], sems.at[0, n * ROW_PARTS + r]),
                pltpu.make_async_copy(g_hbm.at[band, span], g_buf.at[band, span], sems.at[1, n * ROW_PARTS + r]),
            ]
        for copy in pair:
            copy.start()
        large.append(pair)
    for copy in small:
        copy.wait()
    base = base_ref[0]
    by_row, cum = running_sums(decay_ref[...])
    before = scalar_segment(lengths_ref, base - 1)
    last = scalar_segment(lengths_ref, base + rows - 1)
    seg = token_segments(lengths_ref, base + lax.broadcasted_iota(jnp.int32, (rows, heads), 0))
    scale = jnp.where(seg == before, jnp.exp(cum), 0.0)
    factors = split3(jnp.where(last == before, jnp.exp(cum[rows - 1 : rows, :]), 0.0))
    for h in range(heads):
        cols = slice(h * HEAD, (h + 1) * HEAD)
        if (h * HEAD) % width == 0:
            for copy in large[h * HEAD // width]:
                copy.wait()
        scaled = q_buf[:, cols].astype(jnp.float32) * scale[:, h : h + 1]
        hi = scaled.astype(jnp.bfloat16)
        lo = (scaled - hi.astype(jnp.float32)).astype(jnp.bfloat16)
        g_t = g_buf[:, cols].T
        summary = jnp.dot(
            jnp.concatenate([g_t, g_t], axis=1),
            jnp.concatenate([hi, lo], axis=0),
            preferred_element_type=jnp.float32,
        )
        summary = summary.astype(jnp.bfloat16)
        extra = pad_rows([f[:, h : h + 1] for f in factors])
        for part in range(HEAD // HALF):
            slot = h * (HEAD // HALF) + part
            out_ref[slot, 0:HALF, :] = summary[part * HALF : (part + 1) * HALF, :]
            out_ref[slot, HALF : HALF + PAD, :] = extra


def inside_kernel(
    first, base_ref, lengths_ref, q_ref, k_ref, g_ref, decay_ref, after_ref, inside_ref, tail_ref, keys_ref
):
    rows = q_ref.shape[0]
    heads = decay_ref.shape[0]
    base = base_ref[0]
    cum_rows, cum = running_sums(decay_ref[...])
    last = scalar_segment(lengths_ref, base + rows - 1)
    seg = token_segments(lengths_ref, base + lax.broadcasted_iota(jnp.int32, (rows, heads), 0))
    tail_ref[...] = jnp.where(seg == last, jnp.exp(cum[rows - 1 : rows, :] - cum), 0.0)
    i_pos = lax.broadcasted_iota(jnp.int32, (rows, rows), 0)
    t_pos = lax.broadcasted_iota(jnp.int32, (rows, rows), 1)
    same = token_segments(lengths_ref, base + i_pos) == token_segments(lengths_ref, base + t_pos)
    bias = jnp.where(same & (t_pos >= i_pos), 0.0, NEG)
    for n in range(inside_ref.shape[1] // HEAD):
        h = first + n
        cols = slice(h * HEAD, (h + 1) * HEAD)
        here = slice(n * HEAD, (n + 1) * HEAD)
        keys = k_ref[:, cols]
        keys_ref[:, here] = keys
        scores = lax.dot_general(
            keys, q_ref[:, cols], (((1,), (1,)), ((), ())), preferred_element_type=jnp.float32
        )
        gaps = jnp.minimum(cum_rows[h : h + 1, :] - cum[:, h : h + 1], 0.0)
        weights = (jnp.exp(gaps + bias) * scores).astype(jnp.bfloat16)
        inside_ref[:, here] = jnp.dot(weights, g_ref[:, cols], preferred_element_type=jnp.float32)


def factor_row(ref, p):
    tail = ref[p, HALF : HALF + PAD, :].astype(jnp.float32)
    return tail[0:1, :] + tail[1:2, :] + tail[2:3, :]


def write_packet(ref, state, factor):
    size = jnp.abs(state)
    largest = jnp.max(jnp.max(size, axis=0, keepdims=True), axis=1, keepdims=True)
    bound = (largest * 1.01 + TINY).astype(jnp.bfloat16).astype(jnp.float32)
    code = jnp.exp2(size * ((2.0 * OCTAVES) / bound) - OCTAVES)
    ref[0:HALF, :] = jnp.where(state < 0.0, -code, code).astype(jnp.bfloat16)
    ref[HALF : HALF + PAD, :] = pad_rows([bound] + split3(factor))


def read_packet(ref):
    code = ref[0:HALF, :].astype(jnp.float32)
    tail = ref[HALF : HALF + PAD, :].astype(jnp.float32)
    octaves = jnp.log2(jnp.maximum(jnp.abs(code), 2.0**-OCTAVES)) + OCTAVES
    size = octaves * (tail[0:1, :] * (0.5 / OCTAVES))
    return jnp.where(code < 0.0, -size, size), tail[1:2, :] + tail[2:3, :] + tail[3:4, :]


def reduce_kernel(parts_ref, total_ref, factor_ref, packet_ref):
    state = jnp.zeros((HALF, HEAD), jnp.float32)
    factor = jnp.ones((1, HEAD), jnp.float32)
    for p in reversed(range(parts_ref.shape[0])):
        f = factor_row(parts_ref, p)
        state = parts_ref[p, 0:HALF, :].astype(jnp.float32) + f * state
        factor = factor * f
    total_ref[...] = state
    factor_ref[...] = factor
    write_packet(packet_ref, state, factor)


def join(shifts, refs):
    state = jnp.zeros((HALF, HEAD), jnp.float32)
    factor = jnp.ones((1, HEAD), jnp.float32)
    for by, ref in sorted(zip(shifts, refs), key=lambda item: -item[0]):
        s, f = read_packet(ref)
        state = s + f * state
        factor = f * factor
    return state, factor


def join_kernel(total_ref, factor_ref, next_ref, near_ref, near_factor_ref, packet_ref):
    state, factor = read_packet(next_ref)
    near_ref[...] = state
    near_factor_ref[...] = factor
    own = factor_ref[...]
    write_packet(packet_ref, total_ref[...] + own * state, own * factor)


def states_kernel(shifts, after_ref, parts_ref, near_ref, near_factor_ref, *refs):
    out_ref = refs[-1]
    far, far_factor = join(shifts, refs[:-1])
    state = near_ref[...] + near_factor_ref[...] * far
    for p in reversed(range(parts_ref.shape[0])):
        out_ref[p] = state.astype(jnp.bfloat16)
        state = parts_ref[p, 0:HALF, :].astype(jnp.float32) + factor_row(parts_ref, p) * state


def output_kernel(pieces, tail_ref, states_ref, *refs):
    parts = refs[:-3]
    out_hbm, out_buf, sems = refs[-3:]
    owner = [(n, h - first) for n, (first, count) in enumerate(pieces) for h in range(first, first + count)]
    groups = sems.shape[0]
    width = out_buf.shape[1] // groups
    tail = tail_ref[...]
    copies = []
    for h in range(states_ref.shape[0]):
        n, place = owner[h]
        keys_ref, inside_ref = parts[2 * n : 2 * n + 2]
        cols = slice(h * HEAD, (h + 1) * HEAD)
        here = slice(place * HEAD, (place + 1) * HEAD)
        carried = lax.dot_general(
            keys_ref[:, here], states_ref[h], (((1,), (1,)), ((), ())), preferred_element_type=jnp.float32
        )
        out_buf[:, cols] = (inside_ref[:, here] + tail[:, h : h + 1] * carried).astype(jnp.bfloat16)
        if ((h + 1) * HEAD) % width == 0:
            n = h * HEAD // width
            span = slice(n * width, (n + 1) * width)
            copies.append(pltpu.make_async_copy(out_buf.at[:, span], out_hbm.at[:, span], sems.at[n]))
            copies[-1].start()
    for copy in copies:
        copy.wait()


SMEM = pl.BlockSpec(memory_space=pltpu.SMEM)
VMEM = pl.BlockSpec(memory_space=pltpu.VMEM)
REST = pl.BlockSpec(memory_space=pltpu.HBM)


def call(kernel, out_shape, in_specs, args, out_specs=None, scratch=()):
    if out_specs is None:
        out_specs = [VMEM] * len(out_shape) if isinstance(out_shape, (list, tuple)) else VMEM
    return pl.pallas_call(
        kernel,
        out_shape=out_shape,
        in_specs=in_specs,
        out_specs=out_specs,
        scratch_shapes=list(scratch),
        compiler_params=pltpu.CompilerParams(vmem_limit_bytes=40 * 1024 * 1024),
    )(*args)


def from_ahead(x, by):
    size = lax.axis_size("zh")
    return lax.ppermute(x, "zh", [(i + by, i) for i in range(size - by)])


def body(query_vectors, key_vectors, out_grad, log_decay, doc_lengths):
    rows, heads = log_decay.shape
    columns = query_vectors.shape[1]
    slots = columns // HALF
    index = lax.axis_index(("zh",) + GROUP)
    base = (index * rows).astype(jnp.int32).reshape(1)
    decay_rows = log_decay.T
    shape = jax.ShapeDtypeStruct
    dma = pltpu.SemaphoreType.DMA
    pinned = [
        pltpu.with_memory_space_constraint(x, pltpu.HBM) for x in (doc_lengths, query_vectors, out_grad, decay_rows)
    ]
    summaries = call(
        summary_kernel,
        shape((slots, HALF + PAD, HEAD), jnp.bfloat16),
        [SMEM] + [REST] * 4,
        (base, *pinned),
        scratch=(
            pltpu.VMEM((rows, columns), jnp.bfloat16),
            pltpu.VMEM((rows, columns), jnp.bfloat16),
            pltpu.VMEM((heads, rows), jnp.bfloat16),
            pltpu.SMEM(doc_lengths.shape, jnp.int32),
            dma((2, GROUPS * ROW_PARTS)),
            dma((2,)),
        ),
    )
    parts = lax.all_to_all(summaries, GROUP, split_axis=0, concat_axis=0, tiled=True)
    state = shape((HALF, HEAD), jnp.float32)
    factor = shape((1, HEAD), jnp.float32)
    packet = shape((HALF + PAD, HEAD), jnp.bfloat16)
    total, total_factor, own = call(reduce_kernel, (state, factor, packet), [VMEM], (parts,))

    count = 1
    edges = [heads * n // count for n in range(count + 1)]
    pieces = tuple((edges[n], edges[n + 1] - edges[n]) for n in range(count))

    def inside_part(number, after):
        first, here = pieces[number]
        return call(
            functools.partial(inside_kernel, first),
            (
                shape((rows, here * HEAD), jnp.float32),
                shape((rows, heads), jnp.float32),
                shape((rows, here * HEAD), jnp.bfloat16),
            ),
            [SMEM] * 2 + [VMEM] * 5,
            (base, doc_lengths, query_vectors, key_vectors, out_grad, decay_rows, after),
        )

    ahead = {by: from_ahead(own, by) for by in FIRST}
    near, near_factor, wide = call(
        join_kernel, (state, factor, packet), [VMEM] * 3, (total, total_factor, ahead.pop(1))
    )
    ahead.update({by: from_ahead(wide, by) for by in SECOND})
    inside, tail, keys = inside_part(0, wide)
    done = [keys, inside]
    shifts = tuple(sorted(ahead))
    states = call(
        functools.partial(states_kernel, shifts),
        shape((slots, HALF, HEAD), jnp.bfloat16),
        [VMEM] * (4 + len(shifts)),
        (tail, parts, near, near_factor, *[ahead[by] for by in shifts]),
    )
    mine = lax.all_to_all(states, GROUP, split_axis=0, concat_axis=0, tiled=True)
    mine = mine.reshape(heads, HEAD, HEAD)
    return call(
        functools.partial(output_kernel, pieces),
        shape((rows, columns), jnp.bfloat16),
        [VMEM] * (2 + len(done)),
        (tail, mine, *done),
        out_specs=REST,
        scratch=(pltpu.VMEM((rows, columns), jnp.bfloat16), dma((GROUPS,))),
    )


def solution(mesh):
    side = 4
    fine = Mesh(
        mesh.devices.reshape(mesh.shape["seq"] // 4, 2, 2, side, mesh.shape["head"] // side), ("zh",) + GROUP
    )
    tokens = P(("zh",) + GROUP, None)
    return jax.shard_map(
        body, mesh=fine, in_specs=(tokens, tokens, tokens, tokens, P()), out_specs=tokens, check_vma=False
    )
```

```python
import functools
import jax
import jax.numpy as jnp
from jax import lax
from jax.experimental import pallas as pl
from jax.experimental.pallas import tpu as pltpu
from jax.sharding import Mesh, PartitionSpec as P

HEAD = 128
PAD = 8
HALF = 64
FIRST = (1, 4, 5, 6, 7)
SECOND = (2,)
ROW_PARTS = 1
NEG = -1e30
TINY = 1e-36
OCTAVES = 120.0
GROUPS = 2
GROUP = ("zl", "core", "x", "y")
PEERS = ("x", "y", "zl", "core")


def token_segments(lengths_ref, positions):
    start = jnp.int32(0)
    total = jnp.zeros(positions.shape, jnp.int32)
    for d in range(lengths_ref.shape[0]):
        total = total + (start <= positions).astype(jnp.int32)
        start = start + lengths_ref[d]
    return total


def scalar_segment(lengths_ref, position):
    start = jnp.int32(0)
    total = jnp.int32(0)
    for d in range(lengths_ref.shape[0]):
        total = total + (start <= position).astype(jnp.int32)
        start = start + lengths_ref[d]
    return total


def running_sums(decay_rows):
    size = decay_rows.shape[1]
    upto = lax.broadcasted_iota(jnp.int32, (size, size), 0) <= lax.broadcasted_iota(jnp.int32, (size, size), 1)
    by_row = jnp.dot(decay_rows, upto.astype(jnp.bfloat16), preferred_element_type=jnp.float32)
    since = lax.broadcasted_iota(jnp.int32, (size, size), 0) >= lax.broadcasted_iota(jnp.int32, (size, size), 1)
    by_col = lax.dot_general(
        since.astype(jnp.bfloat16), decay_rows, (((1,), (1,)), ((), ())), preferred_element_type=jnp.float32
    )
    return by_row, by_col


def split3(value):
    hi = value.astype(jnp.bfloat16)
    rest = value - hi.astype(jnp.float32)
    mid = rest.astype(jnp.bfloat16)
    lo = (rest - mid.astype(jnp.float32)).astype(jnp.bfloat16)
    return [part.astype(jnp.float32) for part in (hi, mid, lo)]


def pad_rows(rows):
    which = lax.broadcasted_iota(jnp.int32, (PAD, HEAD), 0)
    out = jnp.zeros((PAD, HEAD), jnp.float32)
    for number, row in enumerate(rows):
        out = jnp.where(which == number, jnp.broadcast_to(row, (PAD, HEAD)), out)
    return out.astype(jnp.bfloat16)


def summary_kernel(
    base_ref, lengths_hbm, q_hbm, g_hbm, decay_hbm, out_ref, q_buf, g_buf, decay_ref, lengths_ref, sems, small_sems
):
    rows = q_buf.shape[0]
    heads = decay_ref.shape[0]
    groups = sems.shape[1] // ROW_PARTS
    width = q_buf.shape[1] // groups
    small = [
        pltpu.make_async_copy(lengths_hbm, lengths_ref, small_sems.at[0]),
        pltpu.make_async_copy(decay_hbm, decay_ref, small_sems.at[1]),
    ]
    for copy in small:
        copy.start()
    large = []
    for n in range(groups):
        span = slice(n * width, (n + 1) * width)
        pair = []
        for r in range(ROW_PARTS):
            band = slice(r * rows // ROW_PARTS, (r + 1) * rows // ROW_PARTS)
            pair += [
                pltpu.make_async_copy(q_hbm.at[band, span], q_buf.at[band, span], sems.at[0, n * ROW_PARTS + r]),
                pltpu.make_async_copy(g_hbm.at[band, span], g_buf.at[band, span], sems.at[1, n * ROW_PARTS + r]),
            ]
        for copy in pair:
            copy.start()
        large.append(pair)
    for copy in small:
        copy.wait()
    base = base_ref[0]
    by_row, cum = running_sums(decay_ref[...])
    before = scalar_segment(lengths_ref, base - 1)
    last = scalar_segment(lengths_ref, base + rows - 1)
    seg = token_segments(lengths_ref, base + lax.broadcasted_iota(jnp.int32, (rows, heads), 0))
    scale = jnp.where(seg == before, jnp.exp(cum), 0.0)
    factors = split3(jnp.where(last == before, jnp.exp(cum[rows - 1 : rows, :]), 0.0))
    for h in range(heads):
        cols = slice(h * HEAD, (h + 1) * HEAD)
        if (h * HEAD) % width == 0:
            for copy in large[h * HEAD // width]:
                copy.wait()
        scaled = q_buf[:, cols].astype(jnp.float32) * scale[:, h : h + 1]
        hi = scaled.astype(jnp.bfloat16)
        lo = (scaled - hi.astype(jnp.float32)).astype(jnp.bfloat16)
        g_t = g_buf[:, cols].T
        summary = jnp.dot(
            jnp.concatenate([g_t, g_t], axis=1),
            jnp.concatenate([hi, lo], axis=0),
            preferred_element_type=jnp.float32,
        )
        summary = summary.astype(jnp.bfloat16)
        extra = pad_rows([f[:, h : h + 1] for f in factors])
        for part in range(HEAD // HALF):
            slot = h * (HEAD // HALF) + part
            out_ref[slot, 0:HALF, :] = summary[part * HALF : (part + 1) * HALF, :]
            out_ref[slot, HALF : HALF + PAD, :] = extra


def inside_kernel(
    first, base_ref, lengths_ref, q_ref, k_ref, g_ref, decay_ref, after_ref, inside_ref, tail_ref, keys_ref
):
    rows = q_ref.shape[0]
    heads = decay_ref.shape[0]
    base = base_ref[0]
    cum_rows, cum = running_sums(decay_ref[...])
    last = scalar_segment(lengths_ref, base + rows - 1)
    seg = token_segments(lengths_ref, base + lax.broadcasted_iota(jnp.int32, (rows, heads), 0))
    tail_ref[...] = jnp.where(seg == last, jnp.exp(cum[rows - 1 : rows, :] - cum), 0.0)
    i_pos = lax.broadcasted_iota(jnp.int32, (rows, rows), 0)
    t_pos = lax.broadcasted_iota(jnp.int32, (rows, rows), 1)
    same = token_segments(lengths_ref, base + i_pos) == token_segments(lengths_ref, base + t_pos)
    bias = jnp.where(same & (t_pos >= i_pos), 0.0, NEG)
    for n in range(inside_ref.shape[1] // HEAD):
        h = first + n
        cols = slice(h * HEAD, (h + 1) * HEAD)
        here = slice(n * HEAD, (n + 1) * HEAD)
        keys = k_ref[:, cols]
        keys_ref[:, here] = keys
        scores = lax.dot_general(
            keys, q_ref[:, cols], (((1,), (1,)), ((), ())), preferred_element_type=jnp.float32
        )
        gaps = jnp.minimum(cum_rows[h : h + 1, :] - cum[:, h : h + 1], 0.0)
        weights = (jnp.exp(gaps + bias) * scores).astype(jnp.bfloat16)
        inside_ref[:, here] = jnp.dot(weights, g_ref[:, cols], preferred_element_type=jnp.float32)


def peer_order(count):
    planes = 4
    return [(p % (count // planes)) * planes + p // (count // planes) for p in range(count)]


def factor_row(ref, p):
    tail = ref[p, HALF : HALF + PAD, :].astype(jnp.float32)
    return tail[0:1, :] + tail[1:2, :] + tail[2:3, :]


def write_packet(ref, state, factor):
    size = jnp.abs(state)
    largest = jnp.max(jnp.max(size, axis=0, keepdims=True), axis=1, keepdims=True)
    bound = (largest * 1.01 + TINY).astype(jnp.bfloat16).astype(jnp.float32)
    code = jnp.exp2(size * ((2.0 * OCTAVES) / bound) - OCTAVES)
    ref[0:HALF, :] = jnp.where(state < 0.0, -code, code).astype(jnp.bfloat16)
    ref[HALF : HALF + PAD, :] = pad_rows([bound] + split3(factor))


def read_packet(ref):
    code = ref[0:HALF, :].astype(jnp.float32)
    tail = ref[HALF : HALF + PAD, :].astype(jnp.float32)
    octaves = jnp.log2(jnp.maximum(jnp.abs(code), 2.0**-OCTAVES)) + OCTAVES
    size = octaves * (tail[0:1, :] * (0.5 / OCTAVES))
    return jnp.where(code < 0.0, -size, size), tail[1:2, :] + tail[2:3, :] + tail[3:4, :]


def reduce_kernel(parts_ref, total_ref, factor_ref, packet_ref):
    state = jnp.zeros((HALF, HEAD), jnp.float32)
    factor = jnp.ones((1, HEAD), jnp.float32)
    for p in reversed(peer_order(parts_ref.shape[0])):
        f = factor_row(parts_ref, p)
        state = parts_ref[p, 0:HALF, :].astype(jnp.float32) + f * state
        factor = factor * f
    total_ref[...] = state
    factor_ref[...] = factor
    write_packet(packet_ref, state, factor)


def join(shifts, refs):
    state = jnp.zeros((HALF, HEAD), jnp.float32)
    factor = jnp.ones((1, HEAD), jnp.float32)
    for by, ref in sorted(zip(shifts, refs), key=lambda item: -item[0]):
        s, f = read_packet(ref)
        state = s + f * state
        factor = f * factor
    return state, factor


def join_kernel(total_ref, factor_ref, next_ref, near_ref, near_factor_ref, packet_ref):
    state, factor = read_packet(next_ref)
    near_ref[...] = state
    near_factor_ref[...] = factor
    own = factor_ref[...]
    write_packet(packet_ref, total_ref[...] + own * state, own * factor)


def states_kernel(shifts, after_ref, parts_ref, near_ref, near_factor_ref, *refs):
    out_ref = refs[-1]
    far, far_factor = join(shifts, refs[:-1])
    state = near_ref[...] + near_factor_ref[...] * far
    for p in reversed(peer_order(parts_ref.shape[0])):
        out_ref[p] = state.astype(jnp.bfloat16)
        state = parts_ref[p, 0:HALF, :].astype(jnp.float32) + factor_row(parts_ref, p) * state


def output_kernel(pieces, tail_ref, states_ref, *refs):
    parts = refs[:-3]
    out_hbm, out_buf, sems = refs[-3:]
    owner = [(n, h - first) for n, (first, count) in enumerate(pieces) for h in range(first, first + count)]
    groups = sems.shape[0]
    width = out_buf.shape[1] // groups
    tail = tail_ref[...]
    copies = []
    for h in range(states_ref.shape[0]):
        n, place = owner[h]
        keys_ref, inside_ref = parts[2 * n : 2 * n + 2]
        cols = slice(h * HEAD, (h + 1) * HEAD)
        here = slice(place * HEAD, (place + 1) * HEAD)
        carried = lax.dot_general(
            keys_ref[:, here], states_ref[h], (((1,), (1,)), ((), ())), preferred_element_type=jnp.float32
        )
        out_buf[:, cols] = (inside_ref[:, here] + tail[:, h : h + 1] * carried).astype(jnp.bfloat16)
        if ((h + 1) * HEAD) % width == 0:
            n = h * HEAD // width
            span = slice(n * width, (n + 1) * width)
            copies.append(pltpu.make_async_copy(out_buf.at[:, span], out_hbm.at[:, span], sems.at[n]))
            copies[-1].start()
    for copy in copies:
        copy.wait()


SMEM = pl.BlockSpec(memory_space=pltpu.SMEM)
VMEM = pl.BlockSpec(memory_space=pltpu.VMEM)
REST = pl.BlockSpec(memory_space=pltpu.HBM)


def call(kernel, out_shape, in_specs, args, out_specs=None, scratch=()):
    if out_specs is None:
        out_specs = [VMEM] * len(out_shape) if isinstance(out_shape, (list, tuple)) else VMEM
    return pl.pallas_call(
        kernel,
        out_shape=out_shape,
        in_specs=in_specs,
        out_specs=out_specs,
        scratch_shapes=list(scratch),
        compiler_params=pltpu.CompilerParams(vmem_limit_bytes=40 * 1024 * 1024),
    )(*args)


def from_ahead(x, by):
    size = lax.axis_size("zh")
    return lax.ppermute(x, "zh", [(i + by, i) for i in range(size - by)])


def body(query_vectors, key_vectors, out_grad, log_decay, doc_lengths):
    rows, heads = log_decay.shape
    columns = query_vectors.shape[1]
    slots = columns // HALF
    index = lax.axis_index(("zh",) + GROUP)
    base = (index * rows).astype(jnp.int32).reshape(1)
    decay_rows = log_decay.T
    shape = jax.ShapeDtypeStruct
    dma = pltpu.SemaphoreType.DMA
    pinned = [
        pltpu.with_memory_space_constraint(x, pltpu.HBM) for x in (doc_lengths, query_vectors, out_grad, decay_rows)
    ]
    summaries = call(
        summary_kernel,
        shape((slots, HALF + PAD, HEAD), jnp.bfloat16),
        [SMEM] + [REST] * 4,
        (base, *pinned),
        scratch=(
            pltpu.VMEM((rows, columns), jnp.bfloat16),
            pltpu.VMEM((rows, columns), jnp.bfloat16),
            pltpu.VMEM((heads, rows), jnp.bfloat16),
            pltpu.SMEM(doc_lengths.shape, jnp.int32),
            dma((2, GROUPS * ROW_PARTS)),
            dma((2,)),
        ),
    )
    parts = lax.all_to_all(summaries, PEERS, split_axis=0, concat_axis=0, tiled=True)
    state = shape((HALF, HEAD), jnp.float32)
    factor = shape((1, HEAD), jnp.float32)
    packet = shape((HALF + PAD, HEAD), jnp.bfloat16)
    total, total_factor, own = call(reduce_kernel, (state, factor, packet), [VMEM], (parts,))

    count = 1
    edges = [heads * n // count for n in range(count + 1)]
    pieces = tuple((edges[n], edges[n + 1] - edges[n]) for n in range(count))

    def inside_part(number, after):
        first, here = pieces[number]
        return call(
            functools.partial(inside_kernel, first),
            (
                shape((rows, here * HEAD), jnp.float32),
                shape((rows, heads), jnp.float32),
                shape((rows, here * HEAD), jnp.bfloat16),
            ),
            [SMEM] * 2 + [VMEM] * 5,
            (base, doc_lengths, query_vectors, key_vectors, out_grad, decay_rows, after),
        )

    ahead = {by: from_ahead(own, by) for by in FIRST}
    near, near_factor, wide = call(
        join_kernel, (state, factor, packet), [VMEM] * 3, (total, total_factor, ahead.pop(1))
    )
    ahead.update({by: from_ahead(wide, by) for by in SECOND})
    inside, tail, keys = inside_part(0, wide)
    done = [keys, inside]
    shifts = tuple(sorted(ahead))
    states = call(
        functools.partial(states_kernel, shifts),
        shape((slots, HALF, HEAD), jnp.bfloat16),
        [VMEM] * (4 + len(shifts)),
        (tail, parts, near, near_factor, *[ahead[by] for by in shifts]),
    )
    mine = lax.all_to_all(states, PEERS, split_axis=0, concat_axis=0, tiled=True)
    mine = mine.reshape(heads, HEAD, HEAD)
    return call(
        functools.partial(output_kernel, pieces),
        shape((rows, columns), jnp.bfloat16),
        [VMEM] * (2 + len(done)),
        (tail, mine, *done),
        out_specs=REST,
        scratch=(pltpu.VMEM((rows, columns), jnp.bfloat16), dma((GROUPS,))),
    )


def solution(mesh):
    side = 4
    fine = Mesh(
        mesh.devices.reshape(mesh.shape["seq"] // 4, 2, 2, side, mesh.shape["head"] // side), ("zh",) + GROUP
    )
    tokens = P(("zh",) + GROUP, None)
    return jax.shard_map(
        body, mesh=fine, in_specs=(tokens, tokens, tokens, tokens, P()), out_specs=tokens, check_vma=False
    )
```
